256 devices in a mesh: blk: 16 (over x, y_lo, core), rows: 16 (over z, y_hi).
Axes of the slice: x: 4, y: 4 (y_hi: 2, y_lo: 2; y = y_hi * 2 + y_lo), z: 8, core: 2. Of those that a mesh axis runs over, the one named last changes fastest.
Arguments:
- embeddings: bfloat16 [131072, 384], P(('blk', 'rows')), may hold values from -40 to 40
- factors: bfloat16 [16, 384, 384], P('blk'), may hold values from -4 to 4
- centres: bfloat16 [16, 384], P('blk'), may hold values from -3 to 3
- log_prior: bfloat16 [16], P('blk'), may hold values from -1 to 201
Outputs:
- responsibility: float32 [16, 131072], P(None, ('blk', 'rows'))
- counts: float32 [16], replicated
- first_moment: float32 [16, 384], replicated
- second_moment: float32 [16, 384, 384], P('blk')
The draws below stay inside these ranges and needn't reach their ends.
All inputs are finite; a program needn't handle non-finite values.
Results may differ from the reference program's by a relative error of at most 0.0011.
Values may be sent and summed in bfloat16 or wider, within the bound.
A program may use at most 128 MiB of HBM per device.

```python
import math
import jax
import jax.numpy as jnp
from jax import lax

D = 384
K = 16
ROWS = 131072


def draw_embeddings(key, part):
    subkeys = jax.random.split(jax.random.fold_in(key, 11), 1)
    values = jax.random.normal(subkeys[0], (ROWS, D), jnp.float32)
    values = jnp.clip(values, -6.0, 6.0)
    return values.astype(jnp.bfloat16)


def draw_factors(key, part):
    subkeys = jax.random.split(jax.random.fold_in(key, 23), 2)
    diagonal_part = jnp.exp(jax.random.uniform(subkeys[0], (K, D), jnp.float32, math.log(0.7), math.log(1.4)))
    dense_part = jax.random.normal(subkeys[1], (K, D, D), jnp.float32)
    dense_part = dense_part * (0.5 / math.sqrt(D))
    values = dense_part + diagonal_part[:, :, None] * jnp.eye(D, dtype=jnp.float32)[None, :, :]
    return jnp.clip(values, -4.0, 4.0).astype(jnp.bfloat16)


def draw_log_prior(key, part):
    subkeys = jax.random.split(jax.random.fold_in(key, 37), 1)
    values = jax.random.uniform(subkeys[0], (K,), jnp.float32, -1.0, 1.0)
    return values.astype(jnp.bfloat16)


def block_scale(stream_key, shape, shards, smallest, top_value):
    loudness = 1.0
    for position, parts in shards:
        heights = jax.random.uniform(jax.random.fold_in(jax.random.fold_in(stream_key, 6), position), (parts,), jnp.float32, smallest / len(shards), top_value / len(shards))
        loudness = loudness * jnp.repeat(jnp.exp(heights), shape[position] // parts).reshape((-1,) + (1,) * (len(shape) - 1 - position))
    return loudness


def centred(stream_key, extent, width, reach, cuts=(), kind=jnp.bfloat16):
    gain = block_scale(stream_key, extent, cuts, -0.22, 0.18) if cuts else 1.0
    result = jax.random.normal(stream_key, extent, jnp.float32) * width * gain
    return jnp.minimum(jnp.maximum(result, -reach), reach).astype(kind)


def setup_inputs(seed: int = 0) -> dict:
    key_of = jax.random.split(jax.random.key(seed), 5)
    return {
        "embeddings": draw_embeddings(jax.random.fold_in(key_of[4], 71), 0),
        "factors": draw_factors(jax.random.fold_in(key_of[4], 71), 0),
        "centres": centred(key_of[2], (K, D), 0.5, 3.0, ((0, 16),)),
        "log_prior": draw_log_prior(jax.random.fold_in(key_of[4], 71), 0),
    }


half_temper = 0.05


def reference(embeddings, factors, centres, log_prior):
    def score_one(packed):
        factor_mat, centre_row, prior_val = packed
        whitened = jnp.dot(embeddings, factor_mat, preferred_element_type=jnp.float32) - centre_row.astype(jnp.float32)
        return prior_val.astype(jnp.float32) - half_temper * jnp.sum(whitened * whitened, axis=1)

    scores = lax.map(score_one, (factors, centres, log_prior))
    peak = jnp.max(scores, axis=0, keepdims=True)
    unnorm = jnp.exp(scores - peak)
    responsibility = unnorm / jnp.sum(unnorm, axis=0, keepdims=True)
    normalizer = K / ROWS
    counts = jnp.sum(responsibility, axis=1) * normalizer
    as_float = embeddings.astype(jnp.float32)
    first_moment = jnp.dot(responsibility, as_float, precision=lax.Precision.HIGHEST, preferred_element_type=jnp.float32) * normalizer

    def second_one(resp_row):
        weighted = resp_row[:, None] * as_float
        return jnp.dot(weighted.T, as_float, precision=lax.Precision.HIGHEST, preferred_element_type=jnp.float32) * normalizer

    second_moment = lax.map(second_one, responsibility)
    return responsibility, counts, first_moment, second_moment
```

```python
import functools

import jax
import jax.numpy as jnp
from jax import lax
from jax.experimental import pallas as pl
from jax.experimental.pallas import tpu as pltpu
from jax.sharding import PartitionSpec as P

MESH = pl.DeviceIdType.MESH
HALF_TEMPER = 0.05
D = 384
N_CH = 2
PIECE = 392
CUT = 200
NX, NY, NZ = 4, 4, 8
ZROWS = 48


def kernel(
    scale,
    emb_ref,
    fac_ref,
    cen_ref,
    pri_ref,
    resp_ref,
    counts_ref,
    first_ref,
    second_ref,
    E,
    ET,
    W,
    WT,
    AUX,
    CC,
    S,
    WH,
    WL,
    M,
    RY,
    F,
    QZ,
    ZR,
    G,
    FA,
    es,
    er,
    fs,
    fr,
    ss,
    sr,
    ys,
    yr,
    zs,
    zr,
    gs,
    gr,
    hs,
    hr,
    bs,
    br,
):
    rows = emb_ref.shape[0]
    rc = rows // N_CH
    hc = rc // 2
    b = lax.axis_index("blk")
    rho = lax.axis_index("rows")
    x, l, c = b // 4, (b // 2) % 2, b % 2
    z, h = rho // 2, rho % 2
    y = h * 2 + l
    j = x * 2 + c
    yp, ym = (y + 1) % 4, (y + 3) % 4

    def dev(dx=0, lv=None, dc=0, zv=None, hv=None):
        xx = (x + dx) % 4
        ll = l if lv is None else lv
        cc = (c + dc) % 2
        zz = z if zv is None else zv
        hh = h if hv is None else hv
        return (xx * 4 + ll * 2 + cc, zz * 2 + hh)

    def ydev(yy):
        return dev(lv=yy % 2, hv=yy // 2)

    group = [(dx, dc) for dx in range(4) for dc in range(2) if (dx, dc) != (0, 0)]
    peers = [dev(dx=dx, dc=dc) for dx, dc in group]
    peers += [dev(dx=dx, dc=dc, lv=1 - l) for dx in range(4) for dc in range(2)]
    peers += [dev(hv=1 - h), dev(hv=1 - h, lv=1 - l)]
    peers += [dev(zv=(z + dz) % NZ) for dz in range(1, NZ)]
    barrier = pltpu.get_barrier_semaphore()
    for p in peers:
        pl.semaphore_signal(barrier, inc=1, device_id=p, device_id_type=MESH)

    pending = []

    def send(src, dst, ssem, rsem, to):
        cp = pltpu.make_async_remote_copy(
            src_ref=src, dst_ref=dst, send_sem=ssem, recv_sem=rsem, device_id=to, device_id_type=MESH
        )
        cp.start()
        pending.append(cp)

    def arrived(dst, ssem, rsem):
        pltpu.make_async_remote_copy(
            src_ref=dst, dst_ref=dst, send_sem=ssem, recv_sem=rsem, device_id=dev(dc=1), device_id_type=MESH
        ).wait_recv()

    def slot_of(dx, dc):
        return ((x + dx) % 4) * 2 + (c + dc) % 2

    def lanes(slot):
        return pl.ds(pl.multiple_of(slot * rc, 128), rc)

    def flip(ch, slot):
        ET[ch, :, lanes(slot)] = E[ch, slot].T

    def score(ch, slot, lv):
        wt = jnp.dot(WT[lv], ET[ch, :, lanes(slot)], preferred_element_type=jnp.float32)
        cc = CC[lv]
        wt = wt - jnp.concatenate([cc] * (rc // 128), axis=1)
        total = jnp.sum(wt * wt, axis=0, keepdims=True)
        S[ch, j, pl.ds(lv, 1), lanes(slot)] = AUX[lv, 1:2, 0:1] - HALF_TEMPER * total

    def ready(lv):
        cen = jnp.broadcast_to(AUX[lv, 0:1, :], (128, D))
        CC[lv] = cen.T

    AUX[l, 0:1, :] = cen_ref[...].astype(jnp.float32)
    AUX[l, 1:2, :] = jnp.broadcast_to(pri_ref[...].astype(jnp.float32), (1, D))
    AUX[l, 2:8, :] = jnp.zeros((6, D), jnp.float32)
    WT[l] = fac_ref[0].T
    ready(l)
    for ch in range(N_CH):
        E[ch, j] = emb_ref[pl.ds(ch * rc, rc), :]
        ET[ch, :, lanes(j)] = emb_ref[pl.ds(ch * rc, rc), :].T
        score(ch, j, l)

    pl.semaphore_wait(barrier, len(peers))

    to_xp, to_xm, to_c = dev(dx=1), dev(dx=3), dev(dc=1)
    PH, NH = pl.ds(0, hc), pl.ds(hc, hc)

    def own_rows(ch, part):
        return emb_ref.at[pl.ds(ch * rc + part * hc, hc), :]

    def send_own(ch):
        send(own_rows(ch, 0), E.at[ch, j, PH, :], es.at[ch, 0], er.at[ch, 0], to_xp)
        send(own_rows(ch, 1), E.at[ch, j, NH, :], es.at[ch, 1], er.at[ch, 1], to_xm)
        send(own_rows(ch, 1), E.at[ch, j, NH, :], es.at[ch, 2], er.at[ch, 2], to_xp)
        send(own_rows(ch, 0), E.at[ch, j, PH, :], es.at[ch, 3], er.at[ch, 3], to_xm)

    def wait_e(ch, k, dx, dc, part):
        arrived(E.at[ch, slot_of(dx, dc), part, :], es.at[ch, k], er.at[ch, k])

    def pass_on(ch, k, dx, part, to):
        ref = E.at[ch, slot_of(dx, 0), part, :]
        send(ref, ref, es.at[ch, k], er.at[ch, k], to)

    def relay_first(ch):
        wait_e(ch, 0, 3, 0, PH)
        pass_on(ch, 4, 3, PH, to_xp)
        wait_e(ch, 1, 1, 0, NH)
        pass_on(ch, 5, 1, NH, to_xm)
        if ch + 1 < N_CH:
            send_own(ch + 1)
        pass_on(ch, 6, 3, PH, to_c)
        pass_on(ch, 7, 1, NH, to_c)

    def relay_second(ch):
        wait_e(ch, 2, 3, 0, NH)
        pass_on(ch, 8, 3, NH, to_c)
        wait_e(ch, 3, 1, 0, PH)
        pass_on(ch, 9, 1, PH, to_c)

    def relay_third(ch):
        wait_e(ch, 4, 2, 0, PH)
        pass_on(ch, 10, 2, PH, to_c)
        wait_e(ch, 5, 2, 0, NH)
        pass_on(ch, 11, 2, NH, to_c)

    def both(ch, slot):
        flip(ch, slot)
        score(ch, slot, l)
        score(ch, slot, 1 - l)

    def near(ch):
        both(ch, slot_of(3, 0))
        both(ch, slot_of(1, 0))
        wait_e(ch, 6, 3, 1, PH)
        wait_e(ch, 8, 3, 1, NH)
        both(ch, slot_of(3, 1))
        wait_e(ch, 7, 1, 1, NH)
        wait_e(ch, 9, 1, 1, PH)
        both(ch, slot_of(1, 1))

    def far(ch):
        both(ch, slot_of(2, 0))
        wait_e(ch, 10, 2, 1, PH)
        wait_e(ch, 11, 2, 1, NH)
        both(ch, slot_of(2, 1))
        for k, (dx, dc) in enumerate(group):
            send(S.at[ch, j], S.at[ch, j], ss.at[ch, k], sr.at[ch, k], dev(dx=dx, dc=dc))

    send_own(0)
    send(fac_ref.at[0], W.at[l], fs.at[0], fr.at[0], dev(lv=1 - l))
    send(AUX.at[l], AUX.at[l], fs.at[1], fr.at[1], dev(lv=1 - l))
    for ch in range(N_CH):
        send(emb_ref.at[pl.ds(ch * rc, rc), :], E.at[ch, j], es.at[ch, 12], er.at[ch, 12], to_c)
    for ch in range(N_CH):
        arrived(E.at[ch, slot_of(0, 1)], es.at[ch, 12], er.at[ch, 12])
        flip(ch, slot_of(0, 1))
        score(ch, slot_of(0, 1), l)

    def soften(ch):
        s = S[ch]
        peak = jnp.max(jnp.max(s, axis=0), axis=0, keepdims=True)
        norm = jnp.sum(jnp.sum(jnp.exp(s - peak[None]), axis=0), axis=0, keepdims=True)
        mine = S[ch, :, :, lanes(j)]
        top = jnp.max(jnp.max(mine, axis=0), axis=0, keepdims=True)
        un = jnp.exp(mine - top[None])
        r = un / jnp.sum(jnp.sum(un, axis=0), axis=0, keepdims=True)[None]
        for xx in range(4):
            for cc in range(2):
                for ll in range(2):
                    k = xx * 4 + ll * 2 + cc
                    resp_ref[k : k + 1, pl.ds(ch * rc, rc)] = r[xx * 2 + cc, ll : ll + 1, :]
        return peak, norm

    def gather_moments(ch, lv, peak, norm):
        n = 8 * rc
        r = jnp.exp(S[ch, j, pl.ds(lv, 1), :] - peak) / norm
        for i in range(8):
            sl = slice(i * rc, (i + 1) * rc)
            ri = jnp.broadcast_to(r[:, sl], (8, rc))
            w = ET[ch, :, sl].astype(jnp.float32) * ri[0:1]
            hi = w.astype(jnp.bfloat16)
            WH[0:D, sl] = hi
            WL[0:D, sl] = (w - hi.astype(jnp.float32)).astype(jnp.bfloat16)
            r16 = jnp.concatenate([ri, ri], axis=0)
            rhi = r16.astype(jnp.bfloat16)
            WH[D : D + 16, sl] = rhi
            WL[D : D + 16, sl] = (r16 - rhi.astype(jnp.float32)).astype(jnp.bfloat16)
        left = E[ch, :, :, 0:256].reshape(n, 256)
        right = E[ch, :, :, 256:384].reshape(n, 128)
        a = jnp.dot(WH[...], left, preferred_element_type=jnp.float32)
        a = a + jnp.dot(WL[...], left, preferred_element_type=jnp.float32)
        d = jnp.dot(WH[256:400, :], right, preferred_element_type=jnp.float32)
        d = d + jnp.dot(WL[256:400, :], right, preferred_element_type=jnp.float32)
        cnt = jnp.broadcast_to(jnp.sum(r, axis=1, keepdims=True), (8, 128))
        sub = lax.broadcasted_iota(jnp.int32, (8, 128), 0)
        aux = jnp.where(
            sub == 0,
            a[D : D + 8, 0:128],
            jnp.where(sub == 1, a[D : D + 8, 128:256], jnp.where(sub == 2, d[128:136, :], cnt)),
        )
        parts = [
            (0, 0, a[0:D, 0:128]),
            (0, D, aux),
            (1, 0, a[128:D, 128:256]),
            (1, 256, d[0:128, :]),
            (1, D, aux),
        ]
        for half, at, val in parts:
            where = pl.ds(at, val.shape[0])
            if ch == 0:
                M[lv, half, where, :] = val
            else:
                M[lv, half, where, :] = M[lv, half, where, :] + val

    relay_first(0)
    arrived(AUX.at[1 - l], fs.at[1], fr.at[1])
    arrived(W.at[1 - l], fs.at[0], fr.at[0])
    WT[1 - l] = W[1 - l].T
    ready(1 - l)
    for ch in range(N_CH):
        score(ch, j, 1 - l)
        score(ch, slot_of(0, 1), 1 - l)
    relay_second(0)
    near(0)
    relay_first(1)
    relay_third(0)
    far(0)
    relay_second(1)
    near(1)
    relay_third(1)
    far(1)

    def wait_scores(ch):
        for k, (dx, dc) in enumerate(group):
            arrived(S.at[ch, slot_of(-dx, dc)], ss.at[ch, k], sr.at[ch, k])

    wait_scores(0)
    peak0, norm0 = soften(0)
    gather_moments(0, l, peak0, norm0)
    gather_moments(0, 1 - l, peak0, norm0)
    wait_scores(1)
    peak1, norm1 = soften(1)
    A, B = pl.ds(0, CUT), pl.ds(CUT, PIECE - CUT)
    gather_moments(1, l, peak1, norm1)
    send(M.at[l, 1 - h, A, :], RY.at[A, :], ys.at[0], yr.at[0], ydev(yp))
    send(M.at[l, 1 - h, B, :], RY.at[B, :], ys.at[1], yr.at[1], ydev(ym))
    gather_moments(1, 1 - l, peak1, norm1)
    hp, hm = yp // 2, ym // 2
    send(M.at[1 - l, hp, B, :], F.at[0, B, :], ys.at[2], yr.at[2], ydev(yp))
    send(M.at[1 - l, hm, A, :], F.at[1, A, :], ys.at[3], yr.at[3], ydev(ym))
    arrived(RY.at[A, :], ys.at[0], yr.at[0])
    M[1 - l, hp, A, :] = M[1 - l, hp, A, :] + RY[A, :]
    send(M.at[1 - l, hp, A, :], F.at[0, A, :], ys.at[4], yr.at[4], ydev(yp))
    arrived(RY.at[B, :], ys.at[1], yr.at[1])
    M[1 - l, hm, B, :] = M[1 - l, hm, B, :] + RY[B, :]
    send(M.at[1 - l, hm, B, :], F.at[1, B, :], ys.at[5], yr.at[5], ydev(ym))
    arrived(F.at[0, B, :], ys.at[2], yr.at[2])
    arrived(F.at[1, A, :], ys.at[3], yr.at[3])
    arrived(F.at[0, A, :], ys.at[4], yr.at[4])
    arrived(F.at[1, B, :], ys.at[5], yr.at[5])
    tail = M[l, h, D:PIECE, :] + F[0, D:PIECE, :] + F[1, D:PIECE, :]
    for k in range(NZ):
        sl = slice(k * ZROWS, (k + 1) * ZROWS)
        QZ[k, 0:ZROWS, :] = M[l, h, sl, :] + F[0, sl, :] + F[1, sl, :]
        QZ[k, ZROWS : ZROWS + 8, :] = tail

    for dz in range(1, NZ):
        zz = (z + dz) % NZ
        send(QZ.at[zz], ZR.at[dz - 1], zs.at[dz - 1], zr.at[dz - 1], dev(zv=zz))
    acc = QZ[z]
    for dz in range(1, NZ):
        arrived(ZR.at[dz - 1], zs.at[dz - 1], zr.at[dz - 1])
        acc = acc + ZR[dz - 1]
    acc = acc * scale
    G[h, z] = acc[0:ZROWS]
    FA[b] = acc[ZROWS : ZROWS + 8]
    for dz in range(1, NZ):
        send(G.at[h, z], G.at[h, z], gs.at[dz - 1], gr.at[dz - 1], dev(zv=(z + dz) % NZ))
    over = dev(hv=1 - h)
    send(G.at[h, z], G.at[h, z], hs.at[0], hr.at[0], over)
    blk_peers = [(dl, dx, dc) for dl in range(2) for dx in range(4) for dc in range(2)][1:]
    for k, (dl, dx, dc) in enumerate(blk_peers):
        send(FA.at[b], FA.at[b], bs.at[k], br.at[k], dev(dx=dx, dc=dc, lv=(l + dl) % 2))
    for dz in range(1, NZ):
        zz = (z + NZ - dz) % NZ
        arrived(G.at[h, zz], gs.at[dz - 1], gr.at[dz - 1])
        send(G.at[h, zz], G.at[h, zz], hs.at[dz], hr.at[dz], over)
    for k, (dl, dx, dc) in enumerate(blk_peers):
        bb = ((x - dx) % 4) * 4 + ((l + dl) % 2) * 2 + (c + dc) % 2
        arrived(FA.at[bb], bs.at[k], br.at[k])
    lane = lax.broadcasted_iota(jnp.int32, (1, 16), 1)
    row = jnp.zeros((1, 16), jnp.float32)
    for k in range(16):
        row = jnp.where(lane == k, FA[k, 3:4, 0:16], row)
        for t in range(3):
            first_ref[k : k + 1, t * 128 : (t + 1) * 128] = FA[k, t : t + 1, :]
    counts_ref[...] = row
    for dz in range(NZ):
        zz = (z + NZ - dz) % NZ
        arrived(G.at[1 - h, zz], hs.at[dz], hr.at[dz])
    left = G[0].reshape(D, 128)
    right = G[1].reshape(D, 128)
    second_ref[0, :, 0:128] = left
    second_ref[0, 0:128, 128:256] = left[128:256].T
    second_ref[0, 0:128, 256:384] = left[256:384].T
    second_ref[0, 128:384, 128:256] = right[0:256]
    second_ref[0, 128:256, 256:384] = right[128:256].T
    second_ref[0, 256:384, 256:384] = right[256:384]
    for cp in pending:
        cp.wait_send()


def shards(embeddings, factors, centres, log_prior):
    rows, width = embeddings.shape
    n_comp = factors.shape[0] * lax.axis_size("blk")
    n_rows = lax.axis_size("rows")
    scale = n_comp / (rows * lax.axis_size("blk") * n_rows)
    rc = rows // N_CH
    bf, f32 = jnp.bfloat16, jnp.float32
    vm = pl.BlockSpec(memory_space=pltpu.VMEM)
    dma = pltpu.SemaphoreType.DMA
    resp, counts, first, second = pl.pallas_call(
        functools.partial(kernel, scale),
        out_shape=(
            jax.ShapeDtypeStruct((n_comp, rows), f32),
            jax.ShapeDtypeStruct((1, n_comp), f32),
            jax.ShapeDtypeStruct((n_comp, width), f32),
            jax.ShapeDtypeStruct((1, width, width), f32),
        ),
        in_specs=[vm] * 4,
        out_specs=(vm,) * 4,
        scratch_shapes=[
            pltpu.VMEM((N_CH, 8, rc, width), bf),
            pltpu.VMEM((N_CH, width, 8 * rc), bf),
            pltpu.VMEM((2, width, width), bf),
            pltpu.VMEM((2, width, width), bf),
            pltpu.VMEM((2, 8, width), f32),
            pltpu.VMEM((2, width, 128), f32),
            pltpu.VMEM((N_CH, 8, 2, 8 * rc), f32),
            pltpu.VMEM((width + 16, 8 * rc), bf),
            pltpu.VMEM((width + 16, 8 * rc), bf),
            pltpu.VMEM((2, 2, PIECE, 128), f32),
            pltpu.VMEM((PIECE, 128), f32),
            pltpu.VMEM((2, PIECE, 128), f32),
            pltpu.VMEM((NZ, ZROWS + 8, 128), f32),
            pltpu.VMEM((NZ - 1, ZROWS + 8, 128), f32),
            pltpu.VMEM((2, NZ, ZROWS, 128), f32),
            pltpu.VMEM((16, 8, 128), f32),
            dma((N_CH, 13)),
            dma((N_CH, 13)),
            dma((2,)),
            dma((2,)),
            dma((N_CH, 7)),
            dma((N_CH, 7)),
            dma((6,)),
            dma((6,)),
            dma((NZ - 1,)),
            dma((NZ - 1,)),
            dma((NZ - 1,)),
            dma((NZ - 1,)),
            dma((NZ,)),
            dma((NZ,)),
            dma((15,)),
            dma((15,)),
        ],
        compiler_params=pltpu.CompilerParams(
            collective_id=0, has_side_effects=True, vmem_limit_bytes=56 * 1024 * 1024
        ),
    )(embeddings, factors, centres, log_prior.reshape(1, 1))
    return (resp, counts.reshape(n_comp), first, second)


def solution(mesh):
    in_specs = (P(("blk", "rows"), None), P("blk", None, None), P("blk", None), P("blk"))
    out_specs = (P(None, ("blk", "rows")), P(), P(), P("blk", None, None))
    return jax.shard_map(shards, mesh=mesh, in_specs=in_specs, out_specs=out_specs, check_vma=False)
```

```python
import functools

import jax
import jax.numpy as jnp
from jax import lax
from jax.experimental import pallas as pl
from jax.experimental.pallas import tpu as pltpu
from jax.sharding import PartitionSpec as P

MESH = pl.DeviceIdType.MESH
HALF_TEMPER = 0.05
D = 384
N_CH = 2
PIECE = 328
CUT = 168
BODY = 320
NX, NY, NZ = 4, 4, 8
ZROWS = 40


def kernel(
    scale,
    emb_ref,
    fac_ref,
    cen_ref,
    pri_ref,
    resp_ref,
    aux_ref,
    tri_ref,
    E,
    ET,
    W,
    WT,
    AUX,
    CC,
    S,
    WH,
    WL,
    M,
    RY,
    F,
    QZ,
    ZR,
    G,
    FA,
    es,
    er,
    fs,
    fr,
    ss,
    sr,
    ys,
    yr,
    zs,
    zr,
    gs,
    gr,
    hs,
    hr,
    bs,
    br,
    ls,
):
    rows = emb_ref.shape[0]
    rc = rows // N_CH
    hc = rc // 2
    b = lax.axis_index("blk")
    rho = lax.axis_index("rows")
    x, l, c = b // 4, (b // 2) % 2, b % 2
    z, h = rho // 2, rho % 2
    y = h * 2 + l
    j = x * 2 + c
    yp, ym = (y + 1) % 4, (y + 3) % 4

    def dev(dx=0, lv=None, dc=0, zv=None, hv=None):
        xx = (x + dx) % 4
        ll = l if lv is None else lv
        cc = (c + dc) % 2
        zz = z if zv is None else zv
        hh = h if hv is None else hv
        return (xx * 4 + ll * 2 + cc, zz * 2 + hh)

    def ydev(yy):
        return dev(lv=yy % 2, hv=yy // 2)

    group = [(dx, dc) for dx in range(4) for dc in range(2) if (dx, dc) != (0, 0)]
    peers = [dev(dx=dx, dc=dc) for dx, dc in group]
    peers += [dev(dx=dx, dc=dc, lv=1 - l) for dx in range(4) for dc in range(2)]
    peers += [dev(hv=1 - h), dev(hv=1 - h, lv=1 - l)]
    peers += [dev(zv=(z + dz) % NZ) for dz in range(1, NZ)]
    barrier = pltpu.get_barrier_semaphore()
    for p in peers:
        pl.semaphore_signal(barrier, inc=1, device_id=p, device_id_type=MESH)

    local = [pltpu.make_async_copy(fac_ref.at[0], W.at[l], ls.at[N_CH])]
    for ch in range(N_CH):
        local.append(pltpu.make_async_copy(emb_ref.at[pl.ds(ch * rc, rc), :], E.at[ch, j], ls.at[ch]))
    for cp in local:
        cp.start()

    pending = []

    def send(src, dst, ssem, rsem, to):
        cp = pltpu.make_async_remote_copy(
            src_ref=src, dst_ref=dst, send_sem=ssem, recv_sem=rsem, device_id=to, device_id_type=MESH
        )
        cp.start()
        pending.append(cp)

    def arrived(dst, ssem, rsem):
        pltpu.make_async_remote_copy(
            src_ref=dst, dst_ref=dst, send_sem=ssem, recv_sem=rsem, device_id=dev(dc=1), device_id_type=MESH
        ).wait_recv()

    def slot_of(dx, dc):
        return ((x + dx) % 4) * 2 + (c + dc) % 2

    def lanes(slot):
        return pl.ds(pl.multiple_of(slot * rc, 128), rc)

    def flip(ch, slot):
        ET[ch, :, lanes(slot)] = E[ch, slot].T

    def score(ch, slot, lv):
        wt = jnp.dot(WT[lv], ET[ch, :, lanes(slot)], preferred_element_type=jnp.float32)
        cc = CC[lv]
        wt = wt - jnp.concatenate([cc] * (rc // 128), axis=1)
        total = jnp.sum(wt * wt, axis=0, keepdims=True)
        S[ch, j, pl.ds(lv, 1), lanes(slot)] = AUX[lv, 1:2, 0:1] - HALF_TEMPER * total

    def ready(lv):
        cen = jnp.broadcast_to(AUX[lv, 0:1, :], (128, D))
        CC[lv] = cen.T

    AUX[l, 0:1, :] = cen_ref[...].astype(jnp.float32)
    AUX[l, 1:2, :] = jnp.broadcast_to(pri_ref[...].astype(jnp.float32), (1, D))
    AUX[l, 2:8, :] = jnp.zeros((6, D), jnp.float32)
    pl.semaphore_wait(barrier, len(peers))

    to_xp, to_xm, to_c = dev(dx=1), dev(dx=3), dev(dc=1)
    PH, NH = pl.ds(0, hc), pl.ds(hc, hc)

    def own_rows(ch, part):
        return emb_ref.at[pl.ds(ch * rc + part * hc, hc), :]

    def send_own(ch):
        send(own_rows(ch, 0), E.at[ch, j, PH, :], es.at[ch, 0], er.at[ch, 0], to_xp)
        send(own_rows(ch, 1), E.at[ch, j, NH, :], es.at[ch, 1], er.at[ch, 1], to_xm)
        send(own_rows(ch, 1), E.at[ch, j, NH, :], es.at[ch, 2], er.at[ch, 2], to_xp)
        send(own_rows(ch, 0), E.at[ch, j, PH, :], es.at[ch, 3], er.at[ch, 3], to_xm)

    def wait_e(ch, k, dx, dc, part):
        arrived(E.at[ch, slot_of(dx, dc), part, :], es.at[ch, k], er.at[ch, k])

    def pass_on(ch, k, dx, part, to):
        ref = E.at[ch, slot_of(dx, 0), part, :]
        send(ref, ref, es.at[ch, k], er.at[ch, k], to)

    def relay_first(ch):
        wait_e(ch, 0, 3, 0, PH)
        pass_on(ch, 4, 3, PH, to_xp)
        wait_e(ch, 1, 1, 0, NH)
        pass_on(ch, 5, 1, NH, to_xm)
        if ch + 1 < N_CH:
            send_own(ch + 1)
        pass_on(ch, 6, 3, PH, to_c)
        pass_on(ch, 7, 1, NH, to_c)

    def relay_second(ch):
        wait_e(ch, 2, 3, 0, NH)
        pass_on(ch, 8, 3, NH, to_c)
        wait_e(ch, 3, 1, 0, PH)
        pass_on(ch, 9, 1, PH, to_c)

    def relay_third(ch):
        wait_e(ch, 4, 2, 0, PH)
        pass_on(ch, 10, 2, PH, to_c)
        wait_e(ch, 5, 2, 0, NH)
        pass_on(ch, 11, 2, NH, to_c)

    def both(ch, slot):
        flip(ch, slot)
        score(ch, slot, l)
        score(ch, slot, 1 - l)

    def chip_lanes(dx):
        return pl.ds(pl.multiple_of(((x + dx) % 4) * (2 * rc), 128), 2 * rc)

    def share(ch, at):
        for k, (dx, dc) in enumerate(group):
            ref = S.at[ch, j, :, chip_lanes(at)]
            send(ref, ref, ss.at[ch, at, k], sr.at[ch, (at - dx) % 4, k], dev(dx=dx, dc=dc))

    def near(ch):
        both(ch, slot_of(3, 0))
        both(ch, slot_of(1, 0))
        wait_e(ch, 6, 3, 1, PH)
        wait_e(ch, 8, 3, 1, NH)
        both(ch, slot_of(3, 1))
        share(ch, 3)
        wait_e(ch, 7, 1, 1, NH)
        wait_e(ch, 9, 1, 1, PH)
        both(ch, slot_of(1, 1))
        share(ch, 1)

    def far(ch):
        both(ch, slot_of(2, 0))
        wait_e(ch, 10, 2, 1, PH)
        wait_e(ch, 11, 2, 1, NH)
        both(ch, slot_of(2, 1))
        share(ch, 2)

    send_own(0)
    send(fac_ref.at[0], W.at[l], fs.at[0], fr.at[0], dev(lv=1 - l))
    send(AUX.at[l], AUX.at[l], fs.at[1], fr.at[1], dev(lv=1 - l))
    for ch in range(N_CH):
        send(emb_ref.at[pl.ds(ch * rc, rc), :], E.at[ch, j], es.at[ch, 12], er.at[ch, 12], to_c)
    for cp in local:
        cp.wait()
    WT[l] = W[l].T
    ready(l)
    for ch in range(N_CH):
        flip(ch, j)
        score(ch, j, l)
    for ch in range(N_CH):
        arrived(E.at[ch, slot_of(0, 1)], es.at[ch, 12], er.at[ch, 12])
        flip(ch, slot_of(0, 1))
        score(ch, slot_of(0, 1), l)

    def soften(ch):
        s = S[ch]
        peak = jnp.max(jnp.max(s, axis=0), axis=0, keepdims=True)
        norm = jnp.sum(jnp.sum(jnp.exp(s - peak[None]), axis=0), axis=0, keepdims=True)
        mine = S[ch, :, :, lanes(j)]
        top = jnp.max(jnp.max(mine, axis=0), axis=0, keepdims=True)
        un = jnp.exp(mine - top[None])
        r = un / jnp.sum(jnp.sum(un, axis=0), axis=0, keepdims=True)[None]
        for xx in range(4):
            for cc in range(2):
                for ll in range(2):
                    k = xx * 4 + ll * 2 + cc
                    resp_ref[k : k + 1, pl.ds(ch * rc, rc)] = r[xx * 2 + cc, ll : ll + 1, :]
        return peak, norm

    def gather_moments(ch, lv, peak, norm):
        n = 8 * rc
        r = jnp.exp(S[ch, j, pl.ds(lv, 1), :] - peak) / norm
        for i in range(8):
            sl = slice(i * rc, (i + 1) * rc)
            ri = jnp.broadcast_to(r[:, sl], (8, rc))
            w = ET[ch, :, sl].astype(jnp.float32) * ri[0:1]
            hi = w.astype(jnp.bfloat16)
            WH[0:D, sl] = hi
            WL[0:D, sl] = (w - hi.astype(jnp.float32)).astype(jnp.bfloat16)
            r16 = jnp.concatenate([ri, ri], axis=0)
            rhi = r16.astype(jnp.bfloat16)
            WH[D : D + 16, sl] = rhi
            WL[D : D + 16, sl] = (r16 - rhi.astype(jnp.float32)).astype(jnp.bfloat16)
        left = E[ch, :, :, 0:256].reshape(n, 256)
        right = E[ch, :, :, 256:384].reshape(n, 128)
        a = jnp.dot(WH[...], left, preferred_element_type=jnp.float32)
        a = a + jnp.dot(WL[...], left, preferred_element_type=jnp.float32)
        d = jnp.dot(WH[256:400, :], right, preferred_element_type=jnp.float32)
        d = d + jnp.dot(WL[256:400, :], right, preferred_element_type=jnp.float32)
        row = lax.broadcasted_iota(jnp.int32, (128, 128), 0)
        col = lax.broadcasted_iota(jnp.int32, (128, 128), 1)
        d0, d1 = a[0:128, 0:128], a[128:256, 128:256]
        mixed = jnp.where(row >= col, d0, d1)
        diag = jnp.broadcast_to(jnp.sum(jnp.where(row == col, d1, 0.0), axis=0, keepdims=True), (8, 128))
        cnt = jnp.broadcast_to(jnp.sum(r, axis=1, keepdims=True), (8, 128))
        sub = lax.broadcasted_iota(jnp.int32, (8, 128), 0)
        aux = jnp.where(
            sub == 0,
            a[D : D + 8, 0:128],
            jnp.where(sub == 1, a[D : D + 8, 128:256], jnp.where(sub == 2, d[128:136, :], jnp.where(sub == 3, cnt, diag))),
        )
        parts = [
            (0, 0, a[128:D, 0:128]),
            (0, 256, mixed[0:64]),
            (0, BODY, aux),
            (1, 0, a[256:D, 128:256]),
            (1, 128, d[0:128, :]),
            (1, 256, mixed[64:128]),
            (1, BODY, aux),
        ]
        for half, at, val in parts:
            where = pl.ds(at, val.shape[0])
            if ch == 0:
                M[lv, half, where, :] = val
            else:
                M[lv, half, where, :] = M[lv, half, where, :] + val

    relay_first(0)
    arrived(AUX.at[1 - l], fs.at[1], fr.at[1])
    arrived(W.at[1 - l], fs.at[0], fr.at[0])
    WT[1 - l] = W[1 - l].T
    ready(1 - l)
    for ch in range(N_CH):
        score(ch, j, 1 - l)
        score(ch, slot_of(0, 1), 1 - l)
        share(ch, 0)
    relay_second(0)
    near(0)
    relay_first(1)
    relay_third(0)
    far(0)
    relay_second(1)
    near(1)
    relay_third(1)
    far(1)

    def wait_scores(ch):
        for at in (0, 1, 3, 2):
            for k, (dx, dc) in enumerate(group):
                arrived(S.at[ch, slot_of(-dx, dc), :, chip_lanes(at)], ss.at[ch, at, k], sr.at[ch, at, k])

    wait_scores(0)
    peak0, norm0 = soften(0)
    gather_moments(0, l, peak0, norm0)
    gather_moments(0, 1 - l, peak0, norm0)
    wait_scores(1)
    peak1, norm1 = soften(1)
    A, B = pl.ds(0, CUT), pl.ds(CUT, PIECE - CUT)
    gather_moments(1, l, peak1, norm1)
    send(M.at[l, 1 - h, A, :], RY.at[A, :], ys.at[0], yr.at[0], ydev(yp))
    send(M.at[l, 1 - h, B, :], RY.at[B, :], ys.at[1], yr.at[1], ydev(ym))
    gather_moments(1, 1 - l, peak1, norm1)
    hp, hm = yp // 2, ym // 2
    send(M.at[1 - l, hp, B, :], F.at[0, B, :], ys.at[2], yr.at[2], ydev(yp))
    send(M.at[1 - l, hm, A, :], F.at[1, A, :], ys.at[3], yr.at[3], ydev(ym))
    arrived(RY.at[A, :], ys.at[0], yr.at[0])
    M[1 - l, hp, A, :] = M[1 - l, hp, A, :] + RY[A, :]
    send(M.at[1 - l, hp, A, :], F.at[0, A, :], ys.at[4], yr.at[4], ydev(yp))
    arrived(RY.at[B, :], ys.at[1], yr.at[1])
    M[1 - l, hm, B, :] = M[1 - l, hm, B, :] + RY[B, :]
    send(M.at[1 - l, hm, B, :], F.at[1, B, :], ys.at[5], yr.at[5], ydev(ym))
    arrived(F.at[0, B, :], ys.at[2], yr.at[2])
    arrived(F.at[1, A, :], ys.at[3], yr.at[3])
    arrived(F.at[0, A, :], ys.at[4], yr.at[4])
    arrived(F.at[1, B, :], ys.at[5], yr.at[5])
    tail = M[l, h, BODY:PIECE, :] + F[0, BODY:PIECE, :] + F[1, BODY:PIECE, :]
    for k in range(NZ):
        sl = slice(k * ZROWS, (k + 1) * ZROWS)
        QZ[k, 0:ZROWS, :] = M[l, h, sl, :] + F[0, sl, :] + F[1, sl, :]
        QZ[k, ZROWS : ZROWS + 8, :] = tail

    for dz in range(1, NZ):
        zz = (z + dz) % NZ
        send(QZ.at[zz], ZR.at[dz - 1], zs.at[dz - 1], zr.at[dz - 1], dev(zv=zz))
    acc = QZ[z]
    for dz in range(1, NZ):
        arrived(ZR.at[dz - 1], zs.at[dz - 1], zr.at[dz - 1])
        acc = acc + ZR[dz - 1]
    acc = acc * scale
    G[h, z] = acc[0:ZROWS]
    FA[b] = acc[ZROWS : ZROWS + 8]
    for dz in range(1, NZ):
        send(G.at[h, z], G.at[h, z], gs.at[dz - 1], gr.at[dz - 1], dev(zv=(z + dz) % NZ))
    over = dev(hv=1 - h)
    send(G.at[h, z], G.at[h, z], hs.at[0], hr.at[0], over)
    blk_peers = [(dl, dx, dc) for dl in range(2) for dx in range(4) for dc in range(2)][1:]
    for k, (dl, dx, dc) in enumerate(blk_peers):
        send(FA.at[b], FA.at[b], bs.at[k], br.at[k], dev(dx=dx, dc=dc, lv=(l + dl) % 2))
    for dz in range(1, NZ):
        zz = (z + NZ - dz) % NZ
        arrived(G.at[h, zz], gs.at[dz - 1], gr.at[dz - 1])
        send(G.at[h, zz], G.at[h, zz], hs.at[dz], hr.at[dz], over)
    for k, (dl, dx, dc) in enumerate(blk_peers):
        bb = ((x - dx) % 4) * 4 + ((l + dl) % 2) * 2 + (c + dc) % 2
        arrived(FA.at[bb], bs.at[k], br.at[k])
    aux_ref[...] = FA[...]
    for dz in range(NZ):
        zz = (z + NZ - dz) % NZ
        arrived(G.at[1 - h, zz], hs.at[dz], hr.at[dz])
    tri_ref[...] = G[...]
    for cp in pending:
        cp.wait_send()


def finish(resp_in, aux_ref, tri_ref, resp_ref, counts_ref, first_ref, second_ref):
    b = lax.axis_index("blk")
    resp_ref[...] = resp_in[...]
    lane = lax.broadcasted_iota(jnp.int32, (1, 16), 1)
    counts = jnp.zeros((1, 16), jnp.float32)
    for k in range(16):
        counts = jnp.where(lane == k, aux_ref[k, 3:4, 0:16], counts)
        for t in range(3):
            first_ref[k : k + 1, t * 128 : (t + 1) * 128] = aux_ref[k, t : t + 1, :]
    counts_ref[...] = counts
    g0 = tri_ref[0].reshape(BODY, 128)
    g1 = tri_ref[1].reshape(BODY, 128)
    row = lax.broadcasted_iota(jnp.int32, (128, 128), 0)
    col = lax.broadcasted_iota(jnp.int32, (128, 128), 1)
    mixed = jnp.concatenate([g0[256:320], g1[256:320]], axis=0)
    turned = mixed.T
    diag = aux_ref[b, 4:5, :]
    second_ref[0, 0:128, 0:128] = jnp.where(row >= col, mixed, turned)
    second_ref[0, 128:384, 0:128] = g0[0:256]
    second_ref[0, 0:128, 128:256] = g0[0:128].T
    second_ref[0, 128:256, 128:256] = jnp.where(row < col, mixed, jnp.where(row > col, turned, diag))
    second_ref[0, 256:384, 128:256] = g1[0:128]
    second_ref[0, 0:128, 256:384] = g0[128:256].T
    second_ref[0, 128:256, 256:384] = g1[0:128].T
    second_ref[0, 256:384, 256:384] = g1[128:256]


def shards(embeddings, factors, centres, log_prior):
    rows, width = embeddings.shape
    n_comp = factors.shape[0] * lax.axis_size("blk")
    n_rows = lax.axis_size("rows")
    scale = n_comp / (rows * lax.axis_size("blk") * n_rows)
    rc = rows // N_CH
    bf, f32 = jnp.bfloat16, jnp.float32
    vm = pl.BlockSpec(memory_space=pltpu.VMEM)
    dma = pltpu.SemaphoreType.DMA
    out = jax.ShapeDtypeStruct
    any_ = pl.BlockSpec(memory_space=pltpu.HBM)
    resp, aux, tri = pl.pallas_call(
        functools.partial(kernel, scale),
        out_shape=(
            out((n_comp, rows), f32),
            out((n_comp, 8, 128), f32),
            out((2, NZ, ZROWS, 128), f32),
        ),
        in_specs=[any_, any_, vm, vm],
        out_specs=(vm,) * 3,
        scratch_shapes=[
            pltpu.VMEM((N_CH, 8, rc, width), bf),
            pltpu.VMEM((N_CH, width, 8 * rc), bf),
            pltpu.VMEM((2, width, width), bf),
            pltpu.VMEM((2, width, width), bf),
            pltpu.VMEM((2, 8, width), f32),
            pltpu.VMEM((2, width, 128), f32),
            pltpu.VMEM((N_CH, 8, 2, 8 * rc), f32),
            pltpu.VMEM((width + 16, 8 * rc), bf),
            pltpu.VMEM((width + 16, 8 * rc), bf),
            pltpu.VMEM((2, 2, PIECE, 128), f32),
            pltpu.VMEM((PIECE, 128), f32),
            pltpu.VMEM((2, PIECE, 128), f32),
            pltpu.VMEM((NZ, ZROWS + 8, 128), f32),
            pltpu.VMEM((NZ - 1, ZROWS + 8, 128), f32),
            pltpu.VMEM((2, NZ, ZROWS, 128), f32),
            pltpu.VMEM((16, 8, 128), f32),
            dma((N_CH, 13)),
            dma((N_CH, 13)),
            dma((2,)),
            dma((2,)),
            dma((N_CH, 4, 7)),
            dma((N_CH, 4, 7)),
            dma((6,)),
            dma((6,)),
            dma((NZ - 1,)),
            dma((NZ - 1,)),
            dma((NZ - 1,)),
            dma((NZ - 1,)),
            dma((NZ,)),
            dma((NZ,)),
            dma((15,)),
            dma((15,)),
            dma((N_CH + 1,)),
        ],
        compiler_params=pltpu.CompilerParams(
            collective_id=0, has_side_effects=True, vmem_limit_bytes=48 * 1024 * 1024
        ),
    )(embeddings, factors, centres, log_prior.reshape(1, 1))
    resp, counts, first, second = pl.pallas_call(
        finish,
        out_shape=(
            jax.ShapeDtypeStruct((n_comp, rows), f32),
            jax.ShapeDtypeStruct((1, n_comp), f32),
            jax.ShapeDtypeStruct((n_comp, width), f32),
            jax.ShapeDtypeStruct((1, width, width), f32),
        ),
        in_specs=[vm] * 3,
        out_specs=(vm,) * 4,
        compiler_params=pltpu.CompilerParams(vmem_limit_bytes=8 * 1024 * 1024),
    )(resp, aux, tri)
    return (resp, counts.reshape(n_comp), first, second)


def solution(mesh):
    in_specs = (P(("blk", "rows"), None), P("blk", None, None), P("blk", None), P("blk"))
    out_specs = (P(None, ("blk", "rows")), P(), P(), P("blk", None, None))
    return jax.shard_map(shards, mesh=mesh, in_specs=in_specs, out_specs=out_specs, check_vma=False)
```

```python
import functools

import jax
import jax.numpy as jnp
from jax import lax
from jax.experimental import pallas as pl
from jax.experimental.pallas import tpu as pltpu
from jax.sharding import PartitionSpec as P

MESH = pl.DeviceIdType.MESH
HALF_TEMPER = 0.05
D = 384
N_CH = 2
PIECE = 328
BODY = 320
NZ = 8
ORDER = (1, 7, 2, 6, 3, 5, 4)
Z0, Z1 = 24, 16


def kernel(
    scale,
    emb_ref,
    fac_ref,
    cen_ref,
    pri_ref,
    resp_ref,
    aux_ref,
    tri_ref,
    E,
    ET,
    W,
    WT,
    AUX,
    CC,
    S,
    WH,
    WL,
    M,
    RY,
    F,
    QZ0,
    ZR0,
    G0,
    QZ1,
    ZR1,
    G1,
    FA,
    es,
    er,
    fs,
    fr,
    ss,
    sr,
    ys,
    yr,
    zs,
    zr,
    gs,
    gr,
    hs,
    hr,
    bs,
    br,
    ls,
    ts,
):
    rows = emb_ref.shape[0]
    rc = rows // N_CH
    hc = rc // 2
    b = lax.axis_index("blk")
    rho = lax.axis_index("rows")
    x, l, c = b // 4, (b // 2) % 2, b % 2
    z, h = rho // 2, rho % 2
    y = h * 2 + l
    j = x * 2 + c
    yp, ym = (y + 1) % 4, (y + 3) % 4

    def dev(dx=0, lv=None, dc=0, zv=None, hv=None):
        xx = (x + dx) % 4
        ll = l if lv is None else lv
        cc = (c + dc) % 2
        zz = z if zv is None else zv
        hh = h if hv is None else hv
        return (xx * 4 + ll * 2 + cc, zz * 2 + hh)

    def ydev(yy):
        return dev(lv=yy % 2, hv=yy // 2)

    group = [(dx, dc) for dx in range(4) for dc in range(2) if (dx, dc) != (0, 0)]
    peers = [dev(dx=1), dev(dx=3), dev(dc=1), ydev(yp), ydev(ym), dev(zv=(z + 1) % NZ), dev(zv=(z + 7) % NZ)]
    barrier = pltpu.get_barrier_semaphore()
    for p in peers:
        pl.semaphore_signal(barrier, inc=1, device_id=p, device_id_type=MESH)

    local = [pltpu.make_async_copy(fac_ref.at[0], W.at[l], ls.at[N_CH])]
    for ch in range(N_CH):
        local.append(pltpu.make_async_copy(emb_ref.at[pl.ds(ch * rc, rc), :], E.at[ch, j], ls.at[ch]))
    for cp in local:
        cp.start()

    pending = []

    def send(src, dst, ssem, rsem, to):
        cp = pltpu.make_async_remote_copy(
            src_ref=src, dst_ref=dst, send_sem=ssem, recv_sem=rsem, device_id=to, device_id_type=MESH
        )
        cp.start()
        pending.append(cp)

    def arrived(dst, ssem, rsem):
        pltpu.make_async_remote_copy(
            src_ref=dst, dst_ref=dst, send_sem=ssem, recv_sem=rsem, device_id=dev(dc=1), device_id_type=MESH
        ).wait_recv()

    def slot_of(dx, dc):
        return ((x + dx) % 4) * 2 + (c + dc) % 2

    def lanes(slot):
        return pl.ds(pl.multiple_of(slot * rc, 128), rc)

    def flip(ch, slot):
        ET[ch, :, lanes(slot)] = E[ch, slot].T

    def score(ch, slot, lv):
        wt = jnp.dot(WT[lv], ET[ch, :, lanes(slot)], preferred_element_type=jnp.float32)
        cc = CC[lv]
        wt = wt - jnp.concatenate([cc] * (rc // 128), axis=1)
        total = jnp.sum(wt * wt, axis=0, keepdims=True)
        S[ch, j, pl.ds(lv, 1), lanes(slot)] = AUX[lv, 1:2, 0:1] - HALF_TEMPER * total

    def ready(lv):
        cen = jnp.broadcast_to(AUX[lv, 0:1, :], (128, D))
        CC[lv] = cen.T

    AUX[l, 0:1, :] = cen_ref[...].astype(jnp.float32)
    AUX[l, 1:2, :] = jnp.broadcast_to(pri_ref[...].astype(jnp.float32), (1, D))
    AUX[l, 2:8, :] = jnp.zeros((6, D), jnp.float32)
    pl.semaphore_wait(barrier, len(peers))

    to_xp, to_xm, to_c = dev(dx=1), dev(dx=3), dev(dc=1)
    PH, NH = pl.ds(0, hc), pl.ds(hc, hc)

    def own_rows(ch, part):
        return emb_ref.at[pl.ds(ch * rc + part * hc, hc), :]

    def send_own(ch):
        send(own_rows(ch, 0), E.at[ch, j, PH, :], es.at[ch, 0], er.at[ch, 0], to_xp)
        send(own_rows(ch, 1), E.at[ch, j, NH, :], es.at[ch, 1], er.at[ch, 1], to_xm)
        send(own_rows(ch, 1), E.at[ch, j, NH, :], es.at[ch, 2], er.at[ch, 2], to_xp)
        send(own_rows(ch, 0), E.at[ch, j, PH, :], es.at[ch, 3], er.at[ch, 3], to_xm)

    def wait_e(ch, k, dx, dc, part):
        arrived(E.at[ch, slot_of(dx, dc), part, :], es.at[ch, k], er.at[ch, k])

    def pass_on(ch, k, dx, part, to):
        ref = E.at[ch, slot_of(dx, 0), part, :]
        send(ref, ref, es.at[ch, k], er.at[ch, k], to)

    def relay_first(ch):
        wait_e(ch, 0, 3, 0, PH)
        pass_on(ch, 4, 3, PH, to_xp)
        wait_e(ch, 1, 1, 0, NH)
        pass_on(ch, 5, 1, NH, to_xm)
        if ch + 1 < N_CH:
            send_own(ch + 1)
        pass_on(ch, 6, 3, PH, to_c)
        pass_on(ch, 7, 1, NH, to_c)

    def relay_second(ch):
        wait_e(ch, 2, 3, 0, NH)
        pass_on(ch, 8, 3, NH, to_c)
        wait_e(ch, 3, 1, 0, PH)
        pass_on(ch, 9, 1, PH, to_c)

    def relay_third(ch):
        wait_e(ch, 4, 2, 0, PH)
        pass_on(ch, 10, 2, PH, to_c)
        wait_e(ch, 5, 2, 0, NH)
        pass_on(ch, 11, 2, NH, to_c)

    def both(ch, slot):
        flip(ch, slot)
        score(ch, slot, l)
        score(ch, slot, 1 - l)

    def chip_lanes(dx):
        return pl.ds(pl.multiple_of(((x + dx) % 4) * (2 * rc), 128), 2 * rc)

    def share(ch, at):
        for k, (dx, dc) in enumerate(group):
            ref = S.at[ch, j, :, chip_lanes(at)]
            send(ref, ref, ss.at[ch, at, k], sr.at[ch, (at - dx) % 4, k], dev(dx=dx, dc=dc))

    def near(ch):
        both(ch, slot_of(3, 0))
        both(ch, slot_of(1, 0))
        wait_e(ch, 6, 3, 1, PH)
        wait_e(ch, 8, 3, 1, NH)
        both(ch, slot_of(3, 1))
        share(ch, 0)
        share(ch, 3)
        wait_e(ch, 7, 1, 1, NH)
        wait_e(ch, 9, 1, 1, PH)
        both(ch, slot_of(1, 1))
        share(ch, 1)

    def far(ch):
        both(ch, slot_of(2, 0))
        wait_e(ch, 10, 2, 1, PH)
        wait_e(ch, 11, 2, 1, NH)
        both(ch, slot_of(2, 1))
        share(ch, 2)

    send_own(0)
    send(fac_ref.at[0], W.at[l], fs.at[0], fr.at[0], dev(lv=1 - l))
    send(AUX.at[l], AUX.at[l], fs.at[1], fr.at[1], dev(lv=1 - l))
    for ch in range(N_CH):
        send(emb_ref.at[pl.ds(ch * rc, rc), :], E.at[ch, j], es.at[ch, 12], er.at[ch, 12], to_c)
    for cp in local:
        cp.wait()
    WT[l] = W[l].T
    ready(l)
    for ch in range(N_CH):
        flip(ch, j)
        score(ch, j, l)
    for ch in range(N_CH):
        arrived(E.at[ch, slot_of(0, 1)], es.at[ch, 12], er.at[ch, 12])
        flip(ch, slot_of(0, 1))
        score(ch, slot_of(0, 1), l)

    def tell(k):
        for way, step in ((0, 1), (1, 7)):
            pl.semaphore_signal(ts.at[k, way], inc=1, device_id=dev(zv=(z + step) % NZ), device_id_type=MESH)

    def told(k):
        for way in (0, 1):
            pl.semaphore_wait(ts.at[k, way], 1)

    def soften(ch):
        s = S[ch]
        peak = jnp.max(jnp.max(s, axis=0), axis=0, keepdims=True)
        norm = jnp.sum(jnp.sum(jnp.exp(s - peak[None]), axis=0), axis=0, keepdims=True)
        mine = S[ch, :, :, lanes(j)]
        top = jnp.max(jnp.max(mine, axis=0), axis=0, keepdims=True)
        un = jnp.exp(mine - top[None])
        r = un / jnp.sum(jnp.sum(un, axis=0), axis=0, keepdims=True)[None]
        for xx in range(4):
            for cc in range(2):
                for ll in range(2):
                    k = xx * 4 + ll * 2 + cc
                    resp_ref[k : k + 1, pl.ds(ch * rc, rc)] = r[xx * 2 + cc, ll : ll + 1, :]
        return peak, norm

    def gather_moments(ch, lv, peak, norm):
        n = 8 * rc
        r = jnp.exp(S[ch, j, pl.ds(lv, 1), :] - peak) / norm
        for i in range(8):
            sl = slice(i * rc, (i + 1) * rc)
            ri = jnp.broadcast_to(r[:, sl], (8, rc))
            w = ET[ch, :, sl].astype(jnp.float32) * ri[0:1]
            hi = w.astype(jnp.bfloat16)
            WH[0:D, sl] = hi
            WL[0:D, sl] = (w - hi.astype(jnp.float32)).astype(jnp.bfloat16)
            r16 = jnp.concatenate([ri, ri], axis=0)
            rhi = r16.astype(jnp.bfloat16)
            WH[D : D + 16, sl] = rhi
            WL[D : D + 16, sl] = (r16 - rhi.astype(jnp.float32)).astype(jnp.bfloat16)
        left = E[ch, :, :, 0:256].reshape(n, 256)
        right = E[ch, :, :, 256:384].reshape(n, 128)
        a = jnp.dot(WH[...], left, preferred_element_type=jnp.float32)
        a = a + jnp.dot(WL[...], left, preferred_element_type=jnp.float32)
        d = jnp.dot(WH[256:400, :], right, preferred_element_type=jnp.float32)
        d = d + jnp.dot(WL[256:400, :], right, preferred_element_type=jnp.float32)
        row = lax.broadcasted_iota(jnp.int32, (128, 128), 0)
        col = lax.broadcasted_iota(jnp.int32, (128, 128), 1)
        d0, d1 = a[0:128, 0:128], a[128:256, 128:256]
        mixed = jnp.where(row >= col, d0, d1)
        diag = jnp.broadcast_to(jnp.sum(jnp.where(row == col, d1, 0.0), axis=0, keepdims=True), (8, 128))
        cnt = jnp.broadcast_to(jnp.sum(r, axis=1, keepdims=True), (8, 128))
        sub = lax.broadcasted_iota(jnp.int32, (8, 128), 0)
        aux = jnp.where(
            sub == 0,
            a[D : D + 8, 0:128],
            jnp.where(sub == 1, a[D : D + 8, 128:256], jnp.where(sub == 2, d[128:136, :], jnp.where(sub == 3, cnt, diag))),
        )
        parts = [
            (0, 0, a[128:D, 0:128]),
            (0, 256, mixed[0:64]),
            (0, BODY, aux),
            (1, 0, a[256:D, 128:256]),
            (1, 128, d[0:128, :]),
            (1, 256, mixed[64:128]),
            (1, BODY, aux),
        ]
        for half, at, val in parts:
            where = pl.ds(at, val.shape[0])
            if ch == 0:
                M[lv, half, where, :] = val
            else:
                M[lv, half, where, :] = M[lv, half, where, :] + val

    tell(0)
    relay_first(0)
    told(0)
    tell(1)
    arrived(AUX.at[1 - l], fs.at[1], fr.at[1])
    arrived(W.at[1 - l], fs.at[0], fr.at[0])
    WT[1 - l] = W[1 - l].T
    ready(1 - l)
    for ch in range(N_CH):
        score(ch, j, 1 - l)
        score(ch, slot_of(0, 1), 1 - l)
    relay_second(0)
    told(1)
    tell(2)
    near(0)
    relay_first(1)
    told(2)
    relay_third(0)
    far(0)
    relay_second(1)
    near(1)
    relay_third(1)
    far(1)

    def wait_scores(ch):
        for at in (0, 1, 3, 2):
            for k, (dx, dc) in enumerate(group):
                arrived(S.at[ch, slot_of(-dx, dc), :, chip_lanes(at)], ss.at[ch, at, k], sr.at[ch, at, k])

    wait_scores(0)
    peak0, norm0 = soften(0)
    gather_moments(0, l, peak0, norm0)
    gather_moments(0, 1 - l, peak0, norm0)
    wait_scores(1)
    peak1, norm1 = soften(1)
    A1, A2, B1, B2 = pl.ds(0, 96), pl.ds(96, 64), pl.ds(160, 96), pl.ds(256, 72)
    A, B = pl.ds(0, 160), pl.ds(160, PIECE - 160)
    gather_moments(1, l, peak1, norm1)
    for part, up, down in ((0, A1, B1), (1, A2, B2)):
        send(M.at[l, 1 - h, up, :], RY.at[up, :], ys.at[part], yr.at[part], ydev(yp))
        send(M.at[l, 1 - h, down, :], RY.at[down, :], ys.at[2 + part], yr.at[2 + part], ydev(ym))
    gather_moments(1, 1 - l, peak1, norm1)
    hp, hm = yp // 2, ym // 2
    send(M.at[1 - l, hp, B, :], F.at[0, B, :], ys.at[4], yr.at[4], ydev(yp))
    send(M.at[1 - l, hm, A, :], F.at[1, A, :], ys.at[5], yr.at[5], ydev(ym))
    for part, up, down in ((0, A1, B1), (1, A2, B2)):
        arrived(RY.at[up, :], ys.at[part], yr.at[part])
        M[1 - l, hp, up, :] = M[1 - l, hp, up, :] + RY[up, :]
        send(M.at[1 - l, hp, up, :], F.at[0, up, :], ys.at[6 + part], yr.at[6 + part], ydev(yp))
        arrived(RY.at[down, :], ys.at[2 + part], yr.at[2 + part])
        M[1 - l, hm, down, :] = M[1 - l, hm, down, :] + RY[down, :]
        send(M.at[1 - l, hm, down, :], F.at[1, down, :], ys.at[8 + part], yr.at[8 + part], ydev(ym))

    def total(first, size):
        sl = slice(first, first + size)
        return M[l, h, sl, :] + F[0, sl, :] + F[1, sl, :]

    def along_z(part, Q, R):
        for dz in range(1, NZ):
            zz = (z + dz) % NZ
            send(Q.at[zz], R.at[dz - 1], zs.at[part, dz - 1], zr.at[part, dz - 1], dev(zv=zz))

    def summed(part, Q, R):
        acc = Q[z]
        for dz in range(1, NZ):
            arrived(R.at[dz - 1], zs.at[part, dz - 1], zr.at[part, dz - 1])
            acc = acc + R[dz - 1]
        return acc * scale

    over = dev(hv=1 - h)

    def spread(part, G):
        for dz in range(1, NZ):
            send(G.at[h, z], G.at[h, z], gs.at[part, dz - 1], gr.at[part, dz - 1], dev(zv=(z + dz) % NZ))
        send(G.at[h, z], G.at[h, z], hs.at[part, 0], hr.at[part, 0], over)

    def cross(part, G):
        for dz in ORDER:
            zz = (z + NZ - dz) % NZ
            arrived(G.at[h, zz], gs.at[part, dz - 1], gr.at[part, dz - 1])
            send(G.at[h, zz], G.at[h, zz], hs.at[part, dz], hr.at[part, dz], over)

    arrived(F.at[0, B, :], ys.at[4], yr.at[4])
    arrived(F.at[1, A, :], ys.at[5], yr.at[5])
    arrived(F.at[0, A1, :], ys.at[6], yr.at[6])
    arrived(F.at[1, B1, :], ys.at[8], yr.at[8])
    for k in range(NZ):
        QZ0[k] = total((k // 4) * 160 + (k % 4) * Z0, Z0)
    along_z(0, QZ0, ZR0)
    arrived(F.at[0, A2, :], ys.at[7], yr.at[7])
    arrived(F.at[1, B2, :], ys.at[9], yr.at[9])
    tail = total(BODY, PIECE - BODY)
    for k in range(NZ):
        QZ1[k, 0:Z1, :] = total((k // 4) * 160 + 96 + (k % 4) * Z1, Z1)
        QZ1[k, Z1 : Z1 + 8, :] = tail
    along_z(1, QZ1, ZR1)
    G0[h, z] = summed(0, QZ0, ZR0)
    spread(0, G0)
    acc = summed(1, QZ1, ZR1)
    G1[h, z] = acc[0:Z1]
    FA[b] = acc[Z1 : Z1 + 8]
    spread(1, G1)
    blk_peers = [(dl, dx, dc) for dl in range(2) for dx in range(4) for dc in range(2)][1:]
    for k, (dl, dx, dc) in enumerate(blk_peers):
        send(FA.at[b], FA.at[b], bs.at[k], br.at[k], dev(dx=dx, dc=dc, lv=(l + dl) % 2))
    cross(0, G0)
    cross(1, G1)
    for k, (dl, dx, dc) in enumerate(blk_peers):
        bb = ((x - dx) % 4) * 4 + ((l + dl) % 2) * 2 + (c + dc) % 2
        arrived(FA.at[bb], bs.at[k], br.at[k])
    aux_ref[...] = FA[...]
    for part, G in ((0, G0), (1, G1)):
        for dz in range(NZ):
            arrived(G.at[1 - h, (z + NZ - dz) % NZ], hs.at[part, dz], hr.at[part, dz])
    for k in range(2):
        tri_ref[k, 0:96] = G0[k, 0:4].reshape(96, 128)
        tri_ref[k, 96:160] = G1[k, 0:4].reshape(64, 128)
        tri_ref[k, 160:256] = G0[k, 4:8].reshape(96, 128)
        tri_ref[k, 256:320] = G1[k, 4:8].reshape(64, 128)
    for cp in pending:
        cp.wait_send()


def finish(resp_in, aux_ref, tri_ref, resp_ref, counts_ref, first_ref, second_ref):
    b = lax.axis_index("blk")
    resp_ref[...] = resp_in[...]
    lane = lax.broadcasted_iota(jnp.int32, (1, 16), 1)
    counts = jnp.zeros((1, 16), jnp.float32)
    for k in range(16):
        counts = jnp.where(lane == k, aux_ref[k, 3:4, 0:16], counts)
        for t in range(3):
            first_ref[k : k + 1, t * 128 : (t + 1) * 128] = aux_ref[k, t : t + 1, :]
    counts_ref[...] = counts
    g0, g1 = tri_ref[0], tri_ref[1]
    row = lax.broadcasted_iota(jnp.int32, (128, 128), 0)
    col = lax.broadcasted_iota(jnp.int32, (128, 128), 1)
    mixed = jnp.concatenate([g0[256:320], g1[256:320]], axis=0)
    turned = mixed.T
    diag = aux_ref[b, 4:5, :]
    second_ref[0, 0:128, 0:128] = jnp.where(row >= col, mixed, turned)
    second_ref[0, 128:384, 0:128] = g0[0:256]
    second_ref[0, 0:128, 128:256] = g0[0:128].T
    second_ref[0, 128:256, 128:256] = jnp.where(row < col, mixed, jnp.where(row > col, turned, diag))
    second_ref[0, 256:384, 128:256] = g1[0:128]
    second_ref[0, 0:128, 256:384] = g0[128:256].T
    second_ref[0, 128:256, 256:384] = g1[0:128].T
    second_ref[0, 256:384, 256:384] = g1[128:256]


def shards(embeddings, factors, centres, log_prior):
    rows, width = embeddings.shape
    n_comp = factors.shape[0] * lax.axis_size("blk")
    n_rows = lax.axis_size("rows")
    scale = n_comp / (rows * lax.axis_size("blk") * n_rows)
    rc = rows // N_CH
    bf, f32 = jnp.bfloat16, jnp.float32
    vm = pl.BlockSpec(memory_space=pltpu.VMEM)
    dma = pltpu.SemaphoreType.DMA
    out = pltpu.VMEM
    any_ = pl.BlockSpec(memory_space=pltpu.HBM)
    resp, aux, tri = pl.pallas_call(
        functools.partial(kernel, scale),
        out_shape=(
            out((n_comp, rows), f32),
            out((n_comp, 8, 128), f32),
            out((2, BODY, 128), f32),
        ),
        in_specs=[any_, any_, vm, vm],
        out_specs=(vm,) * 3,
        scratch_shapes=[
            pltpu.VMEM((N_CH, 8, rc, width), bf),
            pltpu.VMEM((N_CH, width, 8 * rc), bf),
            pltpu.VMEM((2, width, width), bf),
            pltpu.VMEM((2, width, width), bf),
            pltpu.VMEM((2, 8, width), f32),
            pltpu.VMEM((2, width, 128), f32),
            pltpu.VMEM((N_CH, 8, 2, 8 * rc), f32),
            pltpu.VMEM((width + 16, 8 * rc), bf),
            pltpu.VMEM((width + 16, 8 * rc), bf),
            pltpu.VMEM((2, 2, PIECE, 128), f32),
            pltpu.VMEM((PIECE, 128), f32),
            pltpu.VMEM((2, PIECE, 128), f32),
            pltpu.VMEM((NZ, Z0, 128), f32),
            pltpu.VMEM((NZ - 1, Z0, 128), f32),
            pltpu.VMEM((2, NZ, Z0, 128), f32),
            pltpu.VMEM((NZ, Z1 + 8, 128), f32),
            pltpu.VMEM((NZ - 1, Z1 + 8, 128), f32),
            pltpu.VMEM((2, NZ, Z1, 128), f32),
            pltpu.VMEM((16, 8, 128), f32),
            dma((N_CH, 13)),
            dma((N_CH, 13)),
            dma((2,)),
            dma((2,)),
            dma((N_CH, 4, 7)),
            dma((N_CH, 4, 7)),
            dma((10,)),
            dma((10,)),
            dma((2, NZ - 1)),
            dma((2, NZ - 1)),
            dma((2, NZ - 1)),
            dma((2, NZ - 1)),
            dma((2, NZ)),
            dma((2, NZ)),
            dma((15,)),
            dma((15,)),
            dma((N_CH + 1,)),
            pltpu.SemaphoreType.REGULAR((3, 2)),
        ],
        compiler_params=pltpu.CompilerParams(
            collective_id=0, has_side_effects=True, vmem_limit_bytes=67043328 - 560 * 1024
        ),
    )(embeddings, factors, centres, log_prior.reshape(1, 1))
    resp, counts, first, second = pl.pallas_call(
        finish,
        out_shape=(
            jax.ShapeDtypeStruct((n_comp, rows), f32),
            jax.ShapeDtypeStruct((1, n_comp), f32),
            jax.ShapeDtypeStruct((n_comp, width), f32),
            jax.ShapeDtypeStruct((1, width, width), f32),
        ),
        in_specs=[vm] * 3,
        out_specs=(vm,) * 4,
        compiler_params=pltpu.CompilerParams(vmem_limit_bytes=8 * 1024 * 1024),
    )(resp, aux, tri)
    return (resp, counts.reshape(n_comp), first, second)


def solution(mesh):
    in_specs = (P(("blk", "rows"), None), P("blk", None, None), P("blk", None), P("blk"))
    out_specs = (P(None, ("blk", "rows")), P(), P(), P("blk", None, None))
    return jax.shard_map(shards, mesh=mesh, in_specs=in_specs, out_specs=out_specs, check_vma=False)
```

```python
import functools

import jax
import jax.numpy as jnp
from jax import lax
from jax.experimental import pallas as pl
from jax.experimental.pallas import tpu as pltpu
from jax.sharding import PartitionSpec as P

MESH = pl.DeviceIdType.MESH
HALF_TEMPER = 0.05
D = 384
N_CH = 2
PIECE = 328
BODY = 320
NZ = 8
ORDER = (1, 7, 2, 6, 3, 5, 4)
Z0, Z1 = 24, 16


def kernel(
    scale,
    emb_ref,
    fac_ref,
    cen_hbm,
    pri_hbm,
    resp_ref,
    aux_ref,
    tri_ref,
    E,
    ET,
    W,
    WT,
    AUX,
    CC,
    S,
    WH,
    WL,
    M,
    RY,
    F,
    QZ0,
    ZR0,
    G0,
    QZ1,
    ZR1,
    G1,
    FA,
    es,
    er,
    fs,
    fr,
    ss,
    sr,
    ys,
    yr,
    zs,
    zr,
    gs,
    gr,
    hs,
    hr,
    bs,
    br,
    ls,
    ts,
    cen_ref,
    pri_ref,
):
    rows = emb_ref.shape[0]
    rc = rows // N_CH
    hc = rc // 2
    b = lax.axis_index("blk")
    rho = lax.axis_index("rows")
    x, l, c = b // 4, (b // 2) % 2, b % 2
    z, h = rho // 2, rho % 2
    y = h * 2 + l
    j = x * 2 + c
    yp, ym = (y + 1) % 4, (y + 3) % 4

    def dev(dx=0, lv=None, dc=0, zv=None, hv=None):
        xx = (x + dx) % 4
        ll = l if lv is None else lv
        cc = (c + dc) % 2
        zz = z if zv is None else zv
        hh = h if hv is None else hv
        return (xx * 4 + ll * 2 + cc, zz * 2 + hh)

    def ydev(yy):
        return dev(lv=yy % 2, hv=yy // 2)

    group = [(dx, dc) for dx in range(4) for dc in range(2) if (dx, dc) != (0, 0)]
    peers = [dev(dx=1), dev(dx=3), dev(dc=1), ydev(yp), ydev(ym), dev(zv=(z + 1) % NZ), dev(zv=(z + 7) % NZ)]
    barrier = pltpu.get_barrier_semaphore()
    for p in peers:
        pl.semaphore_signal(barrier, inc=1, device_id=p, device_id_type=MESH)

    small = [
        pltpu.make_async_copy(cen_hbm, cen_ref, ls.at[N_CH + 1]),
        pltpu.make_async_copy(pri_hbm, pri_ref, ls.at[N_CH + 2]),
    ]
    for cp in small:
        cp.start()
    local = [pltpu.make_async_copy(fac_ref.at[0], W.at[l], ls.at[N_CH])]
    for ch in range(N_CH):
        local.append(pltpu.make_async_copy(emb_ref.at[pl.ds(ch * rc, rc), :], E.at[ch, j], ls.at[ch]))
    for cp in local:
        cp.start()

    pending = []

    def send(src, dst, ssem, rsem, to):
        cp = pltpu.make_async_remote_copy(
            src_ref=src, dst_ref=dst, send_sem=ssem, recv_sem=rsem, device_id=to, device_id_type=MESH
        )
        cp.start()
        pending.append(cp)

    def drain(keep=0):
        while len(pending) > keep:
            pending.pop(0).wait_send()

    def arrived(dst, ssem, rsem):
        pltpu.make_async_remote_copy(
            src_ref=dst, dst_ref=dst, send_sem=ssem, recv_sem=rsem, device_id=dev(dc=1), device_id_type=MESH
        ).wait_recv()

    def slot_of(dx, dc):
        return ((x + dx) % 4) * 2 + (c + dc) % 2

    def lanes(slot):
        return pl.ds(pl.multiple_of(slot * rc, 128), rc)

    def flip(ch, slot):
        ET[ch, :, lanes(slot)] = E[ch, slot].T

    def score(ch, slot, lv):
        wt = jnp.dot(WT[lv], ET[ch, :, lanes(slot)], preferred_element_type=jnp.float32)
        cc = CC[lv]
        wt = wt - jnp.concatenate([cc] * (rc // 128), axis=1)
        total = jnp.sum(wt * wt, axis=0, keepdims=True)
        S[ch, j, pl.ds(lv, 1), lanes(slot)] = AUX[lv, 1:2, 0:1] - HALF_TEMPER * total

    def ready(lv):
        cen = jnp.broadcast_to(AUX[lv, 0:1, :], (128, D))
        CC[lv] = cen.T

    for cp in small:
        cp.wait()
    AUX[l, 0:1, :] = cen_ref[...].astype(jnp.float32)
    AUX[l, 1:2, :] = jnp.broadcast_to(pri_ref[...].astype(jnp.float32), (1, D))
    AUX[l, 2:8, :] = jnp.zeros((6, D), jnp.float32)
    pl.semaphore_wait(barrier, len(peers))

    to_xp, to_xm, to_c = dev(dx=1), dev(dx=3), dev(dc=1)
    PH, NH = pl.ds(0, hc), pl.ds(hc, hc)

    def own_rows(ch, part):
        return emb_ref.at[pl.ds(ch * rc + part * hc, hc), :]

    def send_own(ch):
        send(own_rows(ch, 0), E.at[ch, j, PH, :], es.at[ch, 0], er.at[ch, 0], to_xp)
        send(own_rows(ch, 1), E.at[ch, j, NH, :], es.at[ch, 1], er.at[ch, 1], to_xm)
        send(own_rows(ch, 1), E.at[ch, j, NH, :], es.at[ch, 2], er.at[ch, 2], to_xp)
        send(own_rows(ch, 0), E.at[ch, j, PH, :], es.at[ch, 3], er.at[ch, 3], to_xm)

    def wait_e(ch, k, dx, dc, part):
        arrived(E.at[ch, slot_of(dx, dc), part, :], es.at[ch, k], er.at[ch, k])

    def pass_on(ch, k, dx, part, to):
        ref = E.at[ch, slot_of(dx, 0), part, :]
        send(ref, ref, es.at[ch, k], er.at[ch, k], to)

    def relay_first(ch):
        wait_e(ch, 0, 3, 0, PH)
        pass_on(ch, 4, 3, PH, to_xp)
        wait_e(ch, 1, 1, 0, NH)
        pass_on(ch, 5, 1, NH, to_xm)
        if ch + 1 < N_CH:
            send_own(ch + 1)
        pass_on(ch, 6, 3, PH, to_c)
        pass_on(ch, 7, 1, NH, to_c)

    def relay_second(ch):
        wait_e(ch, 2, 3, 0, NH)
        pass_on(ch, 8, 3, NH, to_c)
        wait_e(ch, 3, 1, 0, PH)
        pass_on(ch, 9, 1, PH, to_c)

    def relay_third(ch):
        wait_e(ch, 4, 2, 0, PH)
        pass_on(ch, 10, 2, PH, to_c)
        wait_e(ch, 5, 2, 0, NH)
        pass_on(ch, 11, 2, NH, to_c)

    def both(ch, slot):
        flip(ch, slot)
        score(ch, slot, l)
        score(ch, slot, 1 - l)

    def chip_lanes(dx):
        return pl.ds(pl.multiple_of(((x + dx) % 4) * (2 * rc), 128), 2 * rc)

    def share(ch, at):
        for k, (dx, dc) in enumerate(group):
            ref = S.at[ch, j, :, chip_lanes(at)]
            send(ref, ref, ss.at[ch, at, k], sr.at[ch, (at - dx) % 4, k], dev(dx=dx, dc=dc))

    def near(ch):
        both(ch, slot_of(3, 0))
        both(ch, slot_of(1, 0))
        wait_e(ch, 6, 3, 1, PH)
        wait_e(ch, 8, 3, 1, NH)
        both(ch, slot_of(3, 1))
        share(ch, 0)
        share(ch, 3)
        wait_e(ch, 7, 1, 1, NH)
        wait_e(ch, 9, 1, 1, PH)
        both(ch, slot_of(1, 1))
        share(ch, 1)

    def far(ch):
        both(ch, slot_of(2, 0))
        wait_e(ch, 10, 2, 1, PH)
        wait_e(ch, 11, 2, 1, NH)
        both(ch, slot_of(2, 1))
        share(ch, 2)

    send_own(0)
    send(fac_ref.at[0], W.at[l], fs.at[0], fr.at[0], dev(lv=1 - l))
    send(AUX.at[l], AUX.at[l], fs.at[1], fr.at[1], dev(lv=1 - l))
    for ch in range(N_CH):
        send(emb_ref.at[pl.ds(ch * rc, rc), :], E.at[ch, j], es.at[ch, 12], er.at[ch, 12], to_c)
    for cp in local:
        cp.wait()
    WT[l] = W[l].T
    ready(l)
    for ch in range(N_CH):
        flip(ch, j)
        score(ch, j, l)
    for ch in range(N_CH):
        arrived(E.at[ch, slot_of(0, 1)], es.at[ch, 12], er.at[ch, 12])
        flip(ch, slot_of(0, 1))
        score(ch, slot_of(0, 1), l)

    def tell(k):
        for way, step in ((0, 1), (1, 7)):
            pl.semaphore_signal(ts.at[k, way], inc=1, device_id=dev(zv=(z + step) % NZ), device_id_type=MESH)

    def told(k):
        for way in (0, 1):
            pl.semaphore_wait(ts.at[k, way], 1)

    def soften(ch):
        s = S[ch]
        peak = jnp.max(jnp.max(s, axis=0), axis=0, keepdims=True)
        norm = jnp.sum(jnp.sum(jnp.exp(s - peak[None]), axis=0), axis=0, keepdims=True)
        mine = S[ch, :, :, lanes(j)]
        top = jnp.max(jnp.max(mine, axis=0), axis=0, keepdims=True)
        un = jnp.exp(mine - top[None])
        r = un / jnp.sum(jnp.sum(un, axis=0), axis=0, keepdims=True)[None]
        for xx in range(4):
            for cc in range(2):
                for ll in range(2):
                    k = xx * 4 + ll * 2 + cc
                    resp_ref[k : k + 1, pl.ds(ch * rc, rc)] = r[xx * 2 + cc, ll : ll + 1, :]
        return peak, norm

    def gather_moments(ch, lv, peak, norm):
        n = 8 * rc
        r = jnp.exp(S[ch, j, pl.ds(lv, 1), :] - peak) / norm
        for i in range(8):
            sl = slice(i * rc, (i + 1) * rc)
            ri = jnp.broadcast_to(r[:, sl], (8, rc))
            w = ET[ch, :, sl].astype(jnp.float32) * ri[0:1]
            hi = w.astype(jnp.bfloat16)
            WH[0:D, sl] = hi
            WL[0:D, sl] = (w - hi.astype(jnp.float32)).astype(jnp.bfloat16)
            r16 = jnp.concatenate([ri, ri], axis=0)
            rhi = r16.astype(jnp.bfloat16)
            WH[D : D + 16, sl] = rhi
            WL[D : D + 16, sl] = (r16 - rhi.astype(jnp.float32)).astype(jnp.bfloat16)
        left = E[ch, :, :, 0:256].reshape(n, 256)
        right = E[ch, :, :, 256:384].reshape(n, 128)
        a = jnp.dot(WH[...], left, preferred_element_type=jnp.float32)
        a = a + jnp.dot(WL[...], left, preferred_element_type=jnp.float32)
        d = jnp.dot(WH[256:400, :], right, preferred_element_type=jnp.float32)
        d = d + jnp.dot(WL[256:400, :], right, preferred_element_type=jnp.float32)
        row = lax.broadcasted_iota(jnp.int32, (128, 128), 0)
        col = lax.broadcasted_iota(jnp.int32, (128, 128), 1)
        d0, d1 = a[0:128, 0:128], a[128:256, 128:256]
        mixed = jnp.where(row >= col, d0, d1)
        diag = jnp.broadcast_to(jnp.sum(jnp.where(row == col, d1, 0.0), axis=0, keepdims=True), (8, 128))
        cnt = jnp.broadcast_to(jnp.sum(r, axis=1, keepdims=True), (8, 128))
        sub = lax.broadcasted_iota(jnp.int32, (8, 128), 0)
        aux = jnp.where(
            sub == 0,
            a[D : D + 8, 0:128],
            jnp.where(sub == 1, a[D : D + 8, 128:256], jnp.where(sub == 2, d[128:136, :], jnp.where(sub == 3, cnt, diag))),
        )
        parts = [
            (0, 0, a[128:D, 0:128]),
            (0, 256, mixed[0:64]),
            (0, BODY, aux),
            (1, 0, a[256:D, 128:256]),
            (1, 128, d[0:128, :]),
            (1, 256, mixed[64:128]),
            (1, BODY, aux),
        ]
        for half, at, val in parts:
            where = pl.ds(at, val.shape[0])
            if ch == 0:
                M[lv, half, where, :] = val
            else:
                M[lv, half, where, :] = M[lv, half, where, :] + val

    tell(0)
    relay_first(0)
    told(0)
    tell(1)
    arrived(AUX.at[1 - l], fs.at[1], fr.at[1])
    arrived(W.at[1 - l], fs.at[0], fr.at[0])
    WT[1 - l] = W[1 - l].T
    ready(1 - l)
    for ch in range(N_CH):
        score(ch, j, 1 - l)
        score(ch, slot_of(0, 1), 1 - l)
    relay_second(0)
    told(1)
    tell(2)
    near(0)
    relay_first(1)
    told(2)
    relay_third(0)
    far(0)
    relay_second(1)
    near(1)
    relay_third(1)
    far(1)

    def wait_scores(ch):
        for at in (0, 1, 3, 2):
            for k, (dx, dc) in enumerate(group):
                arrived(S.at[ch, slot_of(-dx, dc), :, chip_lanes(at)], ss.at[ch, at, k], sr.at[ch, at, k])

    wait_scores(0)
    peak0, norm0 = soften(0)
    gather_moments(0, l, peak0, norm0)
    gather_moments(0, 1 - l, peak0, norm0)
    wait_scores(1)
    peak1, norm1 = soften(1)
    early = len(pending)
    A1, A2, B1, B2 = pl.ds(0, 96), pl.ds(96, 64), pl.ds(160, 96), pl.ds(256, 72)
    A, B = pl.ds(0, 160), pl.ds(160, PIECE - 160)
    gather_moments(1, l, peak1, norm1)
    for part, up, down in ((0, A1, B1), (1, A2, B2)):
        send(M.at[l, 1 - h, up, :], RY.at[up, :], ys.at[part], yr.at[part], ydev(yp))
        send(M.at[l, 1 - h, down, :], RY.at[down, :], ys.at[2 + part], yr.at[2 + part], ydev(ym))
    gather_moments(1, 1 - l, peak1, norm1)
    hp, hm = yp // 2, ym // 2
    send(M.at[1 - l, hp, B, :], F.at[0, B, :], ys.at[4], yr.at[4], ydev(yp))
    send(M.at[1 - l, hm, A, :], F.at[1, A, :], ys.at[5], yr.at[5], ydev(ym))
    drain(len(pending) - early)
    for part, up, down in ((0, A1, B1), (1, A2, B2)):
        arrived(RY.at[up, :], ys.at[part], yr.at[part])
        M[1 - l, hp, up, :] = M[1 - l, hp, up, :] + RY[up, :]
        send(M.at[1 - l, hp, up, :], F.at[0, up, :], ys.at[6 + part], yr.at[6 + part], ydev(yp))
        arrived(RY.at[down, :], ys.at[2 + part], yr.at[2 + part])
        M[1 - l, hm, down, :] = M[1 - l, hm, down, :] + RY[down, :]
        send(M.at[1 - l, hm, down, :], F.at[1, down, :], ys.at[8 + part], yr.at[8 + part], ydev(ym))

    def total(first, size):
        sl = slice(first, first + size)
        return M[l, h, sl, :] + F[0, sl, :] + F[1, sl, :]

    def along_z(part, Q, R):
        for dz in range(1, NZ):
            zz = (z + dz) % NZ
            send(Q.at[zz], R.at[dz - 1], zs.at[part, dz - 1], zr.at[part, dz - 1], dev(zv=zz))

    def summed(part, Q, R):
        acc = Q[z]
        for dz in range(1, NZ):
            arrived(R.at[dz - 1], zs.at[part, dz - 1], zr.at[part, dz - 1])
            acc = acc + R[dz - 1]
        return acc * scale

    over = dev(hv=1 - h)

    def spread(part, G):
        for dz in range(1, NZ):
            send(G.at[h, z], G.at[h, z], gs.at[part, dz - 1], gr.at[part, dz - 1], dev(zv=(z + dz) % NZ))
        send(G.at[h, z], G.at[h, z], hs.at[part, 0], hr.at[part, 0], over)

    def cross(part, G):
        for dz in ORDER:
            zz = (z + NZ - dz) % NZ
            arrived(G.at[h, zz], gs.at[part, dz - 1], gr.at[part, dz - 1])
            send(G.at[h, zz], G.at[h, zz], hs.at[part, dz], hr.at[part, dz], over)

    arrived(F.at[0, B, :], ys.at[4], yr.at[4])
    arrived(F.at[1, A, :], ys.at[5], yr.at[5])
    arrived(F.at[0, A1, :], ys.at[6], yr.at[6])
    arrived(F.at[1, B1, :], ys.at[8], yr.at[8])
    for k in range(NZ):
        QZ0[k] = total((k // 4) * 160 + (k % 4) * Z0, Z0)
    along_z(0, QZ0, ZR0)
    arrived(F.at[0, A2, :], ys.at[7], yr.at[7])
    arrived(F.at[1, B2, :], ys.at[9], yr.at[9])
    tail = total(BODY, PIECE - BODY)
    for k in range(NZ):
        QZ1[k, 0:Z1, :] = total((k // 4) * 160 + 96 + (k % 4) * Z1, Z1)
        QZ1[k, Z1 : Z1 + 8, :] = tail
    along_z(1, QZ1, ZR1)
    G0[h, z] = summed(0, QZ0, ZR0)
    spread(0, G0)
    acc = summed(1, QZ1, ZR1)
    G1[h, z] = acc[0:Z1]
    FA[b] = acc[Z1 : Z1 + 8]
    spread(1, G1)
    blk_peers = [(dl, dx, dc) for dl in range(2) for dx in range(4) for dc in range(2)][1:]
    for k, (dl, dx, dc) in enumerate(blk_peers):
        send(FA.at[b], FA.at[b], bs.at[k], br.at[k], dev(dx=dx, dc=dc, lv=(l + dl) % 2))
    drain(2 * NZ + 15)
    cross(0, G0)
    cross(1, G1)
    drain(2 * NZ)
    for k, (dl, dx, dc) in enumerate(blk_peers):
        bb = ((x - dx) % 4) * 4 + ((l + dl) % 2) * 2 + (c + dc) % 2
        arrived(FA.at[bb], bs.at[k], br.at[k])
    aux_ref[...] = FA[...]
    for part, G in ((0, G0), (1, G1)):
        for dz in range(NZ):
            arrived(G.at[1 - h, (z + NZ - dz) % NZ], hs.at[part, dz], hr.at[part, dz])
    for k in range(2):
        tri_ref[k, 0:96] = G0[k, 0:4].reshape(96, 128)
        tri_ref[k, 96:160] = G1[k, 0:4].reshape(64, 128)
        tri_ref[k, 160:256] = G0[k, 4:8].reshape(96, 128)
        tri_ref[k, 256:320] = G1[k, 4:8].reshape(64, 128)
    drain()


def finish(resp_in, aux_ref, tri_ref, resp_ref, counts_ref, first_ref, second_ref):
    b = lax.axis_index("blk")
    resp_ref[...] = resp_in[...]
    lane = lax.broadcasted_iota(jnp.int32, (1, 16), 1)
    counts = jnp.zeros((1, 16), jnp.float32)
    for k in range(16):
        counts = jnp.where(lane == k, aux_ref[k, 3:4, 0:16], counts)
        for t in range(3):
            first_ref[k : k + 1, t * 128 : (t + 1) * 128] = aux_ref[k, t : t + 1, :]
    counts_ref[...] = counts
    g0, g1 = tri_ref[0], tri_ref[1]
    row = lax.broadcasted_iota(jnp.int32, (128, 128), 0)
    col = lax.broadcasted_iota(jnp.int32, (128, 128), 1)
    mixed = jnp.concatenate([g0[256:320], g1[256:320]], axis=0)
    turned = mixed.T
    diag = aux_ref[b, 4:5, :]
    second_ref[0, 0:128, 0:128] = jnp.where(row >= col, mixed, turned)
    second_ref[0, 128:384, 0:128] = g0[0:256]
    second_ref[0, 0:128, 128:256] = g0[0:128].T
    second_ref[0, 128:256, 128:256] = jnp.where(row < col, mixed, jnp.where(row > col, turned, diag))
    second_ref[0, 256:384, 128:256] = g1[0:128]
    second_ref[0, 0:128, 256:384] = g0[128:256].T
    second_ref[0, 128:256, 256:384] = g1[0:128].T
    second_ref[0, 256:384, 256:384] = g1[128:256]


def shards(embeddings, factors, centres, log_prior):
    rows, width = embeddings.shape
    n_comp = factors.shape[0] * lax.axis_size("blk")
    n_rows = lax.axis_size("rows")
    scale = n_comp / (rows * lax.axis_size("blk") * n_rows)
    rc = rows // N_CH
    bf, f32 = jnp.bfloat16, jnp.float32
    vm = pl.BlockSpec(memory_space=pltpu.VMEM)
    dma = pltpu.SemaphoreType.DMA
    out = pltpu.VMEM
    any_ = pl.BlockSpec(memory_space=pltpu.HBM)
    resp, aux, tri = pl.pallas_call(
        functools.partial(kernel, scale),
        out_shape=(
            out((n_comp, rows), f32),
            out((n_comp, 8, 128), f32),
            out((2, BODY, 128), f32),
        ),
        in_specs=[any_] * 4,
        out_specs=(vm,) * 3,
        scratch_shapes=[
            pltpu.VMEM((N_CH, 8, rc, width), bf),
            pltpu.VMEM((N_CH, width, 8 * rc), bf),
            pltpu.VMEM((2, width, width), bf),
            pltpu.VMEM((2, width, width), bf),
            pltpu.VMEM((2, 8, width), f32),
            pltpu.VMEM((2, width, 128), f32),
            pltpu.VMEM((N_CH, 8, 2, 8 * rc), f32),
            pltpu.VMEM((width + 16, 8 * rc), bf),
            pltpu.VMEM((width + 16, 8 * rc), bf),
            pltpu.VMEM((2, 2, PIECE, 128), f32),
            pltpu.VMEM((PIECE, 128), f32),
            pltpu.VMEM((2, PIECE, 128), f32),
            pltpu.VMEM((NZ, Z0, 128), f32),
            pltpu.VMEM((NZ - 1, Z0, 128), f32),
            pltpu.VMEM((2, NZ, Z0, 128), f32),
            pltpu.VMEM((NZ, Z1 + 8, 128), f32),
            pltpu.VMEM((NZ - 1, Z1 + 8, 128), f32),
            pltpu.VMEM((2, NZ, Z1, 128), f32),
            pltpu.VMEM((16, 8, 128), f32),
            dma((N_CH, 13)),
            dma((N_CH, 13)),
            dma((2,)),
            dma((2,)),
            dma((N_CH, 4, 7)),
            dma((N_CH, 4, 7)),
            dma((10,)),
            dma((10,)),
            dma((2, NZ - 1)),
            dma((2, NZ - 1)),
            dma((2, NZ - 1)),
            dma((2, NZ - 1)),
            dma((2, NZ)),
            dma((2, NZ)),
            dma((15,)),
            dma((15,)),
            dma((N_CH + 3,)),
            pltpu.SemaphoreType.REGULAR((3, 2)),
            pltpu.VMEM((1, width), bf),
            pltpu.VMEM((1, 1), bf),
        ],
        compiler_params=pltpu.CompilerParams(
            collective_id=0, has_side_effects=True, vmem_limit_bytes=67043328 - 560 * 1024
        ),
    )(embeddings, factors, centres, log_prior.reshape(1, 1))
    resp, counts, first, second = pl.pallas_call(
        finish,
        out_shape=(
            jax.ShapeDtypeStruct((n_comp, rows), f32),
            jax.ShapeDtypeStruct((1, n_comp), f32),
            jax.ShapeDtypeStruct((n_comp, width), f32),
            jax.ShapeDtypeStruct((1, width, width), f32),
        ),
        in_specs=[vm] * 3,
        out_specs=(vm,) * 4,
        compiler_params=pltpu.CompilerParams(vmem_limit_bytes=8 * 1024 * 1024),
    )(resp, aux, tri)
    return (resp, counts.reshape(n_comp), first, second)


def solution(mesh):
    in_specs = (P(("blk", "rows"), None), P("blk", None, None), P("blk", None), P("blk"))
    out_specs = (P(None, ("blk", "rows")), P(), P(), P("blk", None, None))
    return jax.shard_map(shards, mesh=mesh, in_specs=in_specs, out_specs=out_specs, check_vma=False)
```

```python
import functools

import jax
import jax.numpy as jnp
from jax import lax
from jax.experimental import pallas as pl
from jax.experimental.pallas import tpu as pltpu
from jax.sharding import PartitionSpec as P

MESH = pl.DeviceIdType.MESH
HALF_TEMPER = 0.05
D = 384
N_CH = 2
PIECE = 296
BODY = 288
NZ = 8
ORDER = (1, 7, 2, 6, 3, 5, 4)
FAR_FIRST = ORDER[::-1]
Z0, Z1 = 24, 12


def kernel(
    scale,
    emb_ref,
    fac_ref,
    cen_hbm,
    pri_hbm,
    resp_ref,
    aux_ref,
    tri_ref,
    E,
    ET,
    W,
    WT,
    AUX,
    CC,
    S,
    WH,
    WL,
    M,
    RY,
    F,
    QZ0,
    ZR0,
    G0,
    QZ1,
    ZR1,
    G1,
    FA,
    es,
    er,
    fs,
    fr,
    ss,
    sr,
    ys,
    yr,
    zs,
    zr,
    gs,
    gr,
    hs,
    hr,
    bs,
    br,
    ls,
    ts,
    cen_ref,
    pri_ref,
):
    rows = emb_ref.shape[0]
    rc = rows // N_CH
    hc = rc // 2
    b = lax.axis_index("blk")
    rho = lax.axis_index("rows")
    x, l, c = b // 4, (b // 2) % 2, b % 2
    z, h = rho // 2, rho % 2
    y = h * 2 + l
    j = x * 2 + c
    yp, ym = (y + 1) % 4, (y + 3) % 4

    def dev(dx=0, lv=None, dc=0, zv=None, hv=None):
        xx = (x + dx) % 4
        ll = l if lv is None else lv
        cc = (c + dc) % 2
        zz = z if zv is None else zv
        hh = h if hv is None else hv
        return (xx * 4 + ll * 2 + cc, zz * 2 + hh)

    def ydev(yy):
        return dev(lv=yy % 2, hv=yy // 2)

    group = [(2, 1), (2, 0), (1, 1), (3, 1), (1, 0), (3, 0), (0, 1)]
    peers = [dev(dx=1), dev(dx=3), dev(dc=1), ydev(yp), ydev(ym), dev(zv=(z + 1) % NZ), dev(zv=(z + 7) % NZ)]
    barrier = pltpu.get_barrier_semaphore()
    for p in peers:
        pl.semaphore_signal(barrier, inc=1, device_id=p, device_id_type=MESH)

    small = [
        pltpu.make_async_copy(cen_hbm, cen_ref, ls.at[N_CH + 1]),
        pltpu.make_async_copy(pri_hbm, pri_ref, ls.at[N_CH + 2]),
    ]
    for cp in small:
        cp.start()
    local = [pltpu.make_async_copy(fac_ref.at[0], W.at[l], ls.at[N_CH])]
    for ch in range(N_CH):
        local.append(pltpu.make_async_copy(emb_ref.at[pl.ds(ch * rc, rc), :], E.at[ch, j], ls.at[ch]))
    for cp in local:
        cp.start()

    pending = []

    def send(src, dst, ssem, rsem, to):
        cp = pltpu.make_async_remote_copy(
            src_ref=src, dst_ref=dst, send_sem=ssem, recv_sem=rsem, device_id=to, device_id_type=MESH
        )
        cp.start()
        pending.append(cp)

    def drain(keep=0):
        while len(pending) > keep:
            pending.pop(0).wait_send()

    def arrived(dst, ssem, rsem):
        pltpu.make_async_remote_copy(
            src_ref=dst, dst_ref=dst, send_sem=ssem, recv_sem=rsem, device_id=dev(dc=1), device_id_type=MESH
        ).wait_recv()

    def slot_of(dx, dc):
        return ((x + dx) % 4) * 2 + (c + dc) % 2

    def lanes(slot):
        return pl.ds(pl.multiple_of(slot * rc, 128), rc)

    def flip(ch, slot):
        ET[ch, :, lanes(slot)] = E[ch, slot].T

    def score(ch, slot, lv):
        wt = jnp.dot(WT[lv], ET[ch, :, lanes(slot)], preferred_element_type=jnp.float32)
        cc = CC[lv]
        wt = wt - jnp.concatenate([cc] * (rc // 128), axis=1)
        total = jnp.sum(wt * wt, axis=0, keepdims=True)
        S[ch, j, pl.ds(lv, 1), lanes(slot)] = AUX[lv, 1:2, 0:1] - HALF_TEMPER * total

    def ready(lv):
        cen = jnp.broadcast_to(AUX[lv, 0:1, :], (128, D))
        CC[lv] = cen.T

    for cp in small:
        cp.wait()
    AUX[l, 0:1, :] = cen_ref[...].astype(jnp.float32)
    AUX[l, 1:2, :] = jnp.broadcast_to(pri_ref[...].astype(jnp.float32), (1, D))
    AUX[l, 2:8, :] = jnp.zeros((6, D), jnp.float32)
    pl.semaphore_wait(barrier, len(peers))

    to_xp, to_xm, to_c = dev(dx=1), dev(dx=3), dev(dc=1)
    PH, NH = pl.ds(0, hc), pl.ds(hc, hc)

    def own_rows(ch, part):
        return emb_ref.at[pl.ds(ch * rc + part * hc, hc), :]

    def send_own(ch):
        send(own_rows(ch, 0), E.at[ch, j, PH, :], es.at[ch, 0], er.at[ch, 0], to_xp)
        send(own_rows(ch, 1), E.at[ch, j, NH, :], es.at[ch, 1], er.at[ch, 1], to_xm)
        send(own_rows(ch, 1), E.at[ch, j, NH, :], es.at[ch, 2], er.at[ch, 2], to_xp)
        send(own_rows(ch, 0), E.at[ch, j, PH, :], es.at[ch, 3], er.at[ch, 3], to_xm)

    def wait_e(ch, k, dx, dc, part):
        arrived(E.at[ch, slot_of(dx, dc), part, :], es.at[ch, k], er.at[ch, k])

    def pass_on(ch, k, dx, part, to):
        ref = E.at[ch, slot_of(dx, 0), part, :]
        send(ref, ref, es.at[ch, k], er.at[ch, k], to)

    def relay_first(ch):
        wait_e(ch, 0, 3, 0, PH)
        pass_on(ch, 4, 3, PH, to_xp)
        wait_e(ch, 1, 1, 0, NH)
        pass_on(ch, 5, 1, NH, to_xm)
        if ch + 1 < N_CH:
            send_own(ch + 1)
        pass_on(ch, 6, 3, PH, to_c)
        pass_on(ch, 7, 1, NH, to_c)

    def relay_second(ch):
        wait_e(ch, 2, 3, 0, NH)
        pass_on(ch, 8, 3, NH, to_c)
        wait_e(ch, 3, 1, 0, PH)
        pass_on(ch, 9, 1, PH, to_c)

    def relay_third(ch):
        wait_e(ch, 4, 2, 0, PH)
        pass_on(ch, 10, 2, PH, to_c)
        wait_e(ch, 5, 2, 0, NH)
        pass_on(ch, 11, 2, NH, to_c)

    def both(ch, slot):
        flip(ch, slot)
        score(ch, slot, l)
        score(ch, slot, 1 - l)

    def chip_lanes(dx):
        return pl.ds(pl.multiple_of(((x + dx) % 4) * (2 * rc), 128), 2 * rc)

    def share(ch, at):
        for k, (dx, dc) in enumerate(group):
            ref = S.at[ch, j, :, chip_lanes(at)]
            send(ref, ref, ss.at[ch, at, k], sr.at[ch, (at - dx) % 4, k], dev(dx=dx, dc=dc))

    def near(ch):
        both(ch, slot_of(3, 0))
        both(ch, slot_of(1, 0))
        wait_e(ch, 6, 3, 1, PH)
        wait_e(ch, 8, 3, 1, NH)
        both(ch, slot_of(3, 1))
        share(ch, 0)
        share(ch, 3)
        wait_e(ch, 7, 1, 1, NH)
        wait_e(ch, 9, 1, 1, PH)
        both(ch, slot_of(1, 1))
        share(ch, 1)

    def far(ch):
        both(ch, slot_of(2, 0))
        wait_e(ch, 10, 2, 1, PH)
        wait_e(ch, 11, 2, 1, NH)
        both(ch, slot_of(2, 1))
        share(ch, 2)

    send_own(0)
    send(fac_ref.at[0], W.at[l], fs.at[0], fr.at[0], dev(lv=1 - l))
    send(AUX.at[l], AUX.at[l], fs.at[1], fr.at[1], dev(lv=1 - l))
    for ch in range(N_CH):
        send(emb_ref.at[pl.ds(ch * rc, rc), :], E.at[ch, j], es.at[ch, 12], er.at[ch, 12], to_c)
    for cp in local:
        cp.wait()
    WT[l] = W[l].T
    ready(l)
    for ch in range(N_CH):
        flip(ch, j)
        score(ch, j, l)
    for ch in range(N_CH):
        arrived(E.at[ch, slot_of(0, 1)], es.at[ch, 12], er.at[ch, 12])
        flip(ch, slot_of(0, 1))
        score(ch, slot_of(0, 1), l)

    def tell(k):
        for way, step in ((0, 1), (1, 7)):
            pl.semaphore_signal(ts.at[k, way], inc=1, device_id=dev(zv=(z + step) % NZ), device_id_type=MESH)

    def told(k):
        for way in (0, 1):
            pl.semaphore_wait(ts.at[k, way], 1)

    def soften(ch):
        s = S[ch]
        peak = jnp.max(jnp.max(s, axis=0), axis=0, keepdims=True)
        norm = jnp.sum(jnp.sum(jnp.exp(s - peak[None]), axis=0), axis=0, keepdims=True)
        mine = S[ch, :, :, lanes(j)]
        top = jnp.max(jnp.max(mine, axis=0), axis=0, keepdims=True)
        un = jnp.exp(mine - top[None])
        r = un / jnp.sum(jnp.sum(un, axis=0), axis=0, keepdims=True)[None]
        for xx in range(4):
            for cc in range(2):
                for ll in range(2):
                    k = xx * 4 + ll * 2 + cc
                    resp_ref[k : k + 1, pl.ds(ch * rc, rc)] = r[xx * 2 + cc, ll : ll + 1, :]
        return peak, norm

    def gather_moments(ch, lv, peak, norm):
        n = 8 * rc
        r = jnp.exp(S[ch, j, pl.ds(lv, 1), :] - peak) / norm
        for i in range(8):
            sl = slice(i * rc, (i + 1) * rc)
            ri = jnp.broadcast_to(r[:, sl], (8, rc))
            w = ET[ch, :, sl].astype(jnp.float32) * ri[0:1]
            hi = w.astype(jnp.bfloat16)
            WH[0:D, sl] = hi
            WL[0:D, sl] = (w - hi.astype(jnp.float32)).astype(jnp.bfloat16)
            r16 = jnp.concatenate([ri, ri], axis=0)
            rhi = r16.astype(jnp.bfloat16)
            WH[D : D + 16, sl] = rhi
            WL[D : D + 16, sl] = (r16 - rhi.astype(jnp.float32)).astype(jnp.bfloat16)
        left = E[ch, :, :, 0:256].reshape(n, 256)
        right = E[ch, :, :, 256:384].reshape(n, 128)
        a = jnp.dot(WH[...], left, preferred_element_type=jnp.float32)
        a = a + jnp.dot(WL[...], left, preferred_element_type=jnp.float32)
        d = jnp.dot(WH[256:400, :], right, preferred_element_type=jnp.float32)
        d = d + jnp.dot(WL[256:400, :], right, preferred_element_type=jnp.float32)
        row = lax.broadcasted_iota(jnp.int32, (128, 128), 0)
        col = lax.broadcasted_iota(jnp.int32, (128, 128), 1)
        d0, d1 = a[0:128, 0:128], a[128:256, 128:256]
        mixed = jnp.where(row >= col, d0, d1)
        diag = jnp.broadcast_to(jnp.sum(jnp.where(row == col, d1, 0.0), axis=0, keepdims=True), (8, 128))
        low = d[64:128, :]
        turn = jnp.where(row[0:64] >= col[0:64] - 64, pltpu.roll(d[0:64, :], 64, 1), low)
        pk = jnp.where(col[0:64] < 64, low, turn)
        diag2 = jnp.sum(jnp.where(row[0:64] == col[0:64] - 64, low, 0.0), axis=0, keepdims=True)
        diag2 = jnp.broadcast_to(diag2, (8, 128))
        cnt = jnp.broadcast_to(jnp.sum(r, axis=1, keepdims=True), (8, 128))
        sub = lax.broadcasted_iota(jnp.int32, (8, 128), 0)
        aux = jnp.where(
            sub == 0,
            a[D : D + 8, 0:128],
            jnp.where(sub == 1, a[D : D + 8, 128:256], jnp.where(sub == 2, d[128:136, :], jnp.where(sub == 3, cnt, jnp.where(sub == 4, diag, diag2)))),
        )
        parts = [
            (0, 0, a[128:D, 0:128]),
            (0, 256, pk[0:32]),
            (0, BODY, aux),
            (1, 0, a[256:D, 128:256]),
            (1, 128, mixed),
            (1, 256, pk[32:64]),
            (1, BODY, aux),
        ]
        for half, at, val in parts:
            where = pl.ds(at, val.shape[0])
            if ch == 0:
                M[lv, half, where, :] = val
            else:
                M[lv, half, where, :] = M[lv, half, where, :] + val

    tell(0)
    relay_first(0)
    told(0)
    tell(1)
    arrived(AUX.at[1 - l], fs.at[1], fr.at[1])
    arrived(W.at[1 - l], fs.at[0], fr.at[0])
    WT[1 - l] = W[1 - l].T
    ready(1 - l)
    for ch in range(N_CH):
        score(ch, j, 1 - l)
        score(ch, slot_of(0, 1), 1 - l)
    relay_second(0)
    told(1)
    tell(2)
    near(0)
    relay_first(1)
    told(2)
    relay_third(0)
    far(0)
    relay_second(1)
    near(1)
    relay_third(1)
    far(1)

    def wait_scores(ch):
        for at in (0, 1, 3, 2):
            for k, (dx, dc) in enumerate(group):
                arrived(S.at[ch, slot_of(-dx, dc), :, chip_lanes(at)], ss.at[ch, at, k], sr.at[ch, at, k])

    wait_scores(0)
    peak0, norm0 = soften(0)
    gather_moments(0, l, peak0, norm0)
    gather_moments(0, 1 - l, peak0, norm0)
    wait_scores(1)
    peak1, norm1 = soften(1)
    early = len(pending)
    A1, A2, B1, B2 = pl.ds(0, 96), pl.ds(96, 48), pl.ds(144, 96), pl.ds(240, 56)
    A, B = pl.ds(0, 144), pl.ds(144, PIECE - 144)
    gather_moments(1, l, peak1, norm1)
    for part, up, down in ((0, A1, B1), (1, A2, B2)):
        send(M.at[l, 1 - h, up, :], RY.at[up, :], ys.at[part], yr.at[part], ydev(yp))
        send(M.at[l, 1 - h, down, :], RY.at[down, :], ys.at[2 + part], yr.at[2 + part], ydev(ym))
    gather_moments(1, 1 - l, peak1, norm1)
    hp, hm = yp // 2, ym // 2
    send(M.at[1 - l, hp, B, :], F.at[0, B, :], ys.at[4], yr.at[4], ydev(yp))
    send(M.at[1 - l, hm, A, :], F.at[1, A, :], ys.at[5], yr.at[5], ydev(ym))
    drain(len(pending) - early)
    for part, up, down in ((0, A1, B1), (1, A2, B2)):
        arrived(RY.at[up, :], ys.at[part], yr.at[part])
        M[1 - l, hp, up, :] = M[1 - l, hp, up, :] + RY[up, :]
        send(M.at[1 - l, hp, up, :], F.at[0, up, :], ys.at[6 + part], yr.at[6 + part], ydev(yp))
        arrived(RY.at[down, :], ys.at[2 + part], yr.at[2 + part])
        M[1 - l, hm, down, :] = M[1 - l, hm, down, :] + RY[down, :]
        send(M.at[1 - l, hm, down, :], F.at[1, down, :], ys.at[8 + part], yr.at[8 + part], ydev(ym))

    def total(first, size):
        sl = slice(first, first + size)
        return M[l, h, sl, :] + F[0, sl, :] + F[1, sl, :]

    def along_z(part, Q, R):
        for dz in FAR_FIRST:
            zz = (z + dz) % NZ
            send(Q.at[zz], R.at[dz - 1], zs.at[part, dz - 1], zr.at[part, dz - 1], dev(zv=zz))

    def summed(part, Q, R):
        acc = Q[z]
        for dz in ORDER:
            arrived(R.at[dz - 1], zs.at[part, dz - 1], zr.at[part, dz - 1])
            acc = acc + R[dz - 1]
        return acc * scale

    over = dev(hv=1 - h)

    def spread(part, G):
        for dz in FAR_FIRST:
            send(G.at[h, z], G.at[h, z], gs.at[part, dz - 1], gr.at[part, dz - 1], dev(zv=(z + dz) % NZ))
        send(G.at[h, z], G.at[h, z], hs.at[part, 0], hr.at[part, 0], over)

    def cross(part, G):
        for dz in ORDER:
            zz = (z + NZ - dz) % NZ
            arrived(G.at[h, zz], gs.at[part, dz - 1], gr.at[part, dz - 1])
            send(G.at[h, zz], G.at[h, zz], hs.at[part, dz], hr.at[part, dz], over)

    arrived(F.at[0, B, :], ys.at[4], yr.at[4])
    arrived(F.at[1, A, :], ys.at[5], yr.at[5])
    arrived(F.at[0, A1, :], ys.at[6], yr.at[6])
    arrived(F.at[1, B1, :], ys.at[8], yr.at[8])
    for k in range(NZ):
        QZ0[k] = total((k // 4) * 144 + (k % 4) * Z0, Z0)
    along_z(0, QZ0, ZR0)
    arrived(F.at[0, A2, :], ys.at[7], yr.at[7])
    arrived(F.at[1, B2, :], ys.at[9], yr.at[9])
    tail = total(BODY, PIECE - BODY)
    for k in range(NZ):
        QZ1[k, 0:Z1, :] = total((k // 4) * 144 + 96 + (k % 4) * Z1, Z1)
        QZ1[k, Z1 : Z1 + 8, :] = tail
    along_z(1, QZ1, ZR1)
    G0[h, z] = summed(0, QZ0, ZR0)
    spread(0, G0)
    acc = summed(1, QZ1, ZR1)
    G1[h, z] = acc[0:Z1]
    FA[b] = acc[Z1 : Z1 + 8]
    spread(1, G1)
    blk_peers = [(dl, dx, dc) for dl in range(2) for dx in range(4) for dc in range(2)][1:]
    for k, (dl, dx, dc) in enumerate(blk_peers):
        send(FA.at[b], FA.at[b], bs.at[k], br.at[k], dev(dx=dx, dc=dc, lv=(l + dl) % 2))
    drain(2 * NZ + 15)
    cross(0, G0)
    cross(1, G1)
    drain(2 * NZ)
    for k, (dl, dx, dc) in enumerate(blk_peers):
        bb = ((x - dx) % 4) * 4 + ((l + dl) % 2) * 2 + (c + dc) % 2
        arrived(FA.at[bb], bs.at[k], br.at[k])
    aux_ref[...] = FA[...]
    for part, G in ((0, G0), (1, G1)):
        for dz in range(NZ):
            arrived(G.at[1 - h, (z + NZ - dz) % NZ], hs.at[part, dz], hr.at[part, dz])
    for k in range(2):
        for t in range(NZ):
            at = (t // 4) * 144
            tri_ref[k, at + (t % 4) * Z0 : at + (t % 4 + 1) * Z0] = G0[k, t]
            tri_ref[k, at + 96 + (t % 4) * Z1 : at + 96 + (t % 4 + 1) * Z1] = G1[k, t]
    drain()


def finish(resp_in, aux_ref, tri_ref, resp_ref, counts_ref, first_ref, second_ref):
    b = lax.axis_index("blk")
    resp_ref[...] = resp_in[...]
    lane = lax.broadcasted_iota(jnp.int32, (1, 16), 1)
    counts = jnp.zeros((1, 16), jnp.float32)
    for k in range(16):
        counts = jnp.where(lane == k, aux_ref[k, 3:4, 0:16], counts)
        for t in range(3):
            first_ref[k : k + 1, t * 128 : (t + 1) * 128] = aux_ref[k, t : t + 1, :]
    counts_ref[...] = counts
    g0, g1 = tri_ref[0], tri_ref[1]
    row = lax.broadcasted_iota(jnp.int32, (128, 128), 0)
    col = lax.broadcasted_iota(jnp.int32, (128, 128), 1)
    mixed = g1[128:256]
    pk = jnp.concatenate([g0[256:288], g1[256:288]], axis=0)
    zero = jnp.zeros((64, 128), jnp.float32)
    low = jnp.concatenate([zero, pk], axis=0)
    high = jnp.concatenate([pltpu.roll(pk, 64, 1), zero], axis=0)
    low_t, high_t = low.T, high.T
    diag2 = aux_ref[b, 5:6, :]
    second_block = jnp.where(row < col, low, jnp.where(row > col, low_t, diag2))
    first_block = jnp.where(row >= col, high, high_t)
    bottom = jnp.where(col < 64, low, second_block)
    top = jnp.where(col < 64, first_block, low_t)
    corner = jnp.where(row < 64, top, bottom)
    turned = mixed.T
    diag = aux_ref[b, 4:5, :]
    second_ref[0, 0:128, 0:128] = jnp.where(row >= col, mixed, turned)
    second_ref[0, 128:384, 0:128] = g0[0:256]
    second_ref[0, 0:128, 128:256] = g0[0:128].T
    second_ref[0, 128:256, 128:256] = jnp.where(row < col, mixed, jnp.where(row > col, turned, diag))
    second_ref[0, 256:384, 128:256] = g1[0:128]
    second_ref[0, 0:128, 256:384] = g0[128:256].T
    second_ref[0, 128:256, 256:384] = g1[0:128].T
    second_ref[0, 256:384, 256:384] = corner


def shards(embeddings, factors, centres, log_prior):
    rows, width = embeddings.shape
    n_comp = factors.shape[0] * lax.axis_size("blk")
    n_rows = lax.axis_size("rows")
    scale = n_comp / (rows * lax.axis_size("blk") * n_rows)
    rc = rows // N_CH
    bf, f32 = jnp.bfloat16, jnp.float32
    vm = pl.BlockSpec(memory_space=pltpu.VMEM)
    dma = pltpu.SemaphoreType.DMA
    out = pltpu.VMEM
    any_ = pl.BlockSpec(memory_space=pltpu.HBM)
    resp, aux, tri = pl.pallas_call(
        functools.partial(kernel, scale),
        out_shape=(
            out((n_comp, rows), f32),
            out((n_comp, 8, 128), f32),
            out((2, BODY, 128), f32),
        ),
        in_specs=[any_] * 4,
        out_specs=(vm,) * 3,
        scratch_shapes=[
            pltpu.VMEM((N_CH, 8, rc, width), bf),
            pltpu.VMEM((N_CH, width, 8 * rc), bf),
            pltpu.VMEM((2, width, width), bf),
            pltpu.VMEM((2, width, width), bf),
            pltpu.VMEM((2, 8, width), f32),
            pltpu.VMEM((2, width, 128), f32),
            pltpu.VMEM((N_CH, 8, 2, 8 * rc), f32),
            pltpu.VMEM((width + 16, 8 * rc), bf),
            pltpu.VMEM((width + 16, 8 * rc), bf),
            pltpu.VMEM((2, 2, PIECE, 128), f32),
            pltpu.VMEM((PIECE, 128), f32),
            pltpu.VMEM((2, PIECE, 128), f32),
            pltpu.VMEM((NZ, Z0, 128), f32),
            pltpu.VMEM((NZ - 1, Z0, 128), f32),
            pltpu.VMEM((2, NZ, Z0, 128), f32),
            pltpu.VMEM((NZ, Z1 + 8, 128), f32),
            pltpu.VMEM((NZ - 1, Z1 + 8, 128), f32),
            pltpu.VMEM((2, NZ, Z1, 128), f32),
            pltpu.VMEM((16, 8, 128), f32),
            dma((N_CH, 13)),
            dma((N_CH, 13)),
            dma((2,)),
            dma((2,)),
            dma((N_CH, 4, 7)),
            dma((N_CH, 4, 7)),
            dma((10,)),
            dma((10,)),
            dma((2, NZ - 1)),
            dma((2, NZ - 1)),
            dma((2, NZ - 1)),
            dma((2, NZ - 1)),
            dma((2, NZ)),
            dma((2, NZ)),
            dma((15,)),
            dma((15,)),
            dma((N_CH + 3,)),
            pltpu.SemaphoreType.REGULAR((3, 2)),
            pltpu.VMEM((1, width), bf),
            pltpu.VMEM((1, 1), bf),
        ],
        compiler_params=pltpu.CompilerParams(
            collective_id=0, has_side_effects=True, vmem_limit_bytes=67043328 - 560 * 1024
        ),
    )(embeddings, factors, centres, log_prior.reshape(1, 1))
    resp, counts, first, second = pl.pallas_call(
        finish,
        out_shape=(
            jax.ShapeDtypeStruct((n_comp, rows), f32),
            jax.ShapeDtypeStruct((1, n_comp), f32),
            jax.ShapeDtypeStruct((n_comp, width), f32),
            jax.ShapeDtypeStruct((1, width, width), f32),
        ),
        in_specs=[vm] * 3,
        out_specs=(vm,) * 4,
        compiler_params=pltpu.CompilerParams(vmem_limit_bytes=8 * 1024 * 1024),
    )(resp, aux, tri)
    return (resp, counts.reshape(n_comp), first, second)


def solution(mesh):
    in_specs = (P(("blk", "rows"), None), P("blk", None, None), P("blk", None), P("blk"))
    out_specs = (P(None, ("blk", "rows")), P(), P(), P("blk", None, None))
    return jax.shard_map(shards, mesh=mesh, in_specs=in_specs, out_specs=out_specs, check_vma=False)
```

```python
import functools

import jax
import jax.numpy as jnp
from jax import lax
from jax.experimental import pallas as pl
from jax.experimental.pallas import tpu as pltpu
from jax.sharding import PartitionSpec as P

MESH = pl.DeviceIdType.MESH
HALF_TEMPER = 0.05
D = 384
N_CH = 2
PIECE = 296
BODY = 288
NZ = 8
ORDER = (1, 7, 2, 6, 3, 5, 4)
FAR_FIRST = ORDER[::-1]
Z0, Z1 = 24, 12


def kernel(
    scale,
    emb_ref,
    fac_ref,
    cen_hbm,
    pri_hbm,
    resp_ref,
    aux_ref,
    tri_ref,
    E,
    ET,
    W,
    WT,
    AUX,
    CC,
    S,
    WH,
    WL,
    M,
    RY,
    F,
    QZ0,
    ZR0,
    G0,
    QZ1,
    ZR1,
    G1,
    FA,
    es,
    er,
    fs,
    fr,
    ss,
    sr,
    ys,
    yr,
    zs,
    zr,
    gs,
    gr,
    hs,
    hr,
    bs,
    br,
    ls,
    ts,
    cen_ref,
    pri_ref,
):
    rows = emb_ref.shape[0]
    rc = rows // N_CH
    hc = rc // 2
    b = lax.axis_index("blk")
    rho = lax.axis_index("rows")
    x, l, c = b // 4, (b // 2) % 2, b % 2
    z, h = rho // 2, rho % 2
    y = h * 2 + l
    j = x * 2 + c
    yp, ym = (y + 1) % 4, (y + 3) % 4

    def dev(dx=0, lv=None, dc=0, zv=None, hv=None):
        xx = (x + dx) % 4
        ll = l if lv is None else lv
        cc = (c + dc) % 2
        zz = z if zv is None else zv
        hh = h if hv is None else hv
        return (xx * 4 + ll * 2 + cc, zz * 2 + hh)

    def ydev(yy):
        return dev(lv=yy % 2, hv=yy // 2)

    group = [(2, 1), (2, 0), (1, 1), (3, 1), (1, 0), (3, 0), (0, 1)]
    peers = [dev(dx=1), dev(dx=3), dev(dc=1), ydev(yp), ydev(ym), dev(zv=(z + 1) % NZ), dev(zv=(z + 7) % NZ)]
    barrier = pltpu.get_barrier_semaphore()
    for p in peers:
        pl.semaphore_signal(barrier, inc=1, device_id=p, device_id_type=MESH)

    small = [
        pltpu.make_async_copy(cen_hbm, cen_ref, ls.at[N_CH + 1]),
        pltpu.make_async_copy(pri_hbm, pri_ref, ls.at[N_CH + 2]),
    ]
    for cp in small:
        cp.start()
    local = [pltpu.make_async_copy(fac_ref.at[0], W.at[l], ls.at[N_CH])]
    for ch in range(N_CH):
        local.append(pltpu.make_async_copy(emb_ref.at[pl.ds(ch * rc, rc), :], E.at[ch, j], ls.at[ch]))
    for cp in local:
        cp.start()

    pending = []

    def send(src, dst, ssem, rsem, to):
        cp = pltpu.make_async_remote_copy(
            src_ref=src, dst_ref=dst, send_sem=ssem, recv_sem=rsem, device_id=to, device_id_type=MESH
        )
        cp.start()
        pending.append(cp)

    def drain(keep=0):
        while len(pending) > keep:
            pending.pop(0).wait_send()

    def arrived(dst, ssem, rsem):
        pltpu.make_async_remote_copy(
            src_ref=dst, dst_ref=dst, send_sem=ssem, recv_sem=rsem, device_id=dev(dc=1), device_id_type=MESH
        ).wait_recv()

    def slot_of(dx, dc):
        return ((x + dx) % 4) * 2 + (c + dc) % 2

    def lanes(slot):
        return pl.ds(pl.multiple_of(slot * rc, 128), rc)

    def flip(ch, slot):
        ET[ch, :, lanes(slot)] = E[ch, slot].T

    def score(ch, slot, lv):
        wt = jnp.dot(WT[lv], ET[ch, :, lanes(slot)], preferred_element_type=jnp.float32)
        cc = CC[lv]
        wt = wt - jnp.concatenate([cc] * (rc // 128), axis=1)
        total = jnp.sum(wt * wt, axis=0, keepdims=True)
        S[ch, j, pl.ds(lv, 1), lanes(slot)] = AUX[lv, 1:2, 0:1] - HALF_TEMPER * total

    def ready(lv):
        cen = jnp.broadcast_to(AUX[lv, 0:1, :], (128, D))
        CC[lv] = cen.T

    for cp in small:
        cp.wait()
    AUX[l, 0:1, :] = cen_ref[...].astype(jnp.float32)
    AUX[l, 1:2, :] = jnp.broadcast_to(pri_ref[...].astype(jnp.float32), (1, D))
    AUX[l, 2:8, :] = jnp.zeros((6, D), jnp.float32)
    pl.semaphore_wait(barrier, len(peers))

    to_xp, to_xm, to_c = dev(dx=1), dev(dx=3), dev(dc=1)
    PH, NH = pl.ds(0, hc), pl.ds(hc, hc)

    def own_rows(ch, part):
        return emb_ref.at[pl.ds(ch * rc + part * hc, hc), :]

    def send_own(ch):
        send(own_rows(ch, 0), E.at[ch, j, PH, :], es.at[ch, 0], er.at[ch, 0], to_xp)
        send(own_rows(ch, 1), E.at[ch, j, NH, :], es.at[ch, 1], er.at[ch, 1], to_xm)
        send(own_rows(ch, 1), E.at[ch, j, NH, :], es.at[ch, 2], er.at[ch, 2], to_xp)
        send(own_rows(ch, 0), E.at[ch, j, PH, :], es.at[ch, 3], er.at[ch, 3], to_xm)

    def wait_e(ch, k, dx, dc, part):
        arrived(E.at[ch, slot_of(dx, dc), part, :], es.at[ch, k], er.at[ch, k])

    def pass_on(ch, k, dx, part, to):
        ref = E.at[ch, slot_of(dx, 0), part, :]
        send(ref, ref, es.at[ch, k], er.at[ch, k], to)

    def relay_first(ch):
        wait_e(ch, 0, 3, 0, PH)
        pass_on(ch, 4, 3, PH, to_xp)
        wait_e(ch, 1, 1, 0, NH)
        pass_on(ch, 5, 1, NH, to_xm)
        if ch + 1 < N_CH:
            send_own(ch + 1)
        pass_on(ch, 6, 3, PH, to_c)
        pass_on(ch, 7, 1, NH, to_c)

    def relay_second(ch):
        wait_e(ch, 2, 3, 0, NH)
        pass_on(ch, 8, 3, NH, to_c)
        wait_e(ch, 3, 1, 0, PH)
        pass_on(ch, 9, 1, PH, to_c)

    def relay_third(ch):
        wait_e(ch, 4, 2, 0, PH)
        pass_on(ch, 10, 2, PH, to_c)
        wait_e(ch, 5, 2, 0, NH)
        pass_on(ch, 11, 2, NH, to_c)

    def both(ch, slot):
        flip(ch, slot)
        score(ch, slot, l)
        score(ch, slot, 1 - l)

    def chip_lanes(dx):
        return pl.ds(pl.multiple_of(((x + dx) % 4) * (2 * rc), 128), 2 * rc)

    def share(ch, at):
        for k, (dx, dc) in enumerate(group):
            ref = S.at[ch, j, :, chip_lanes(at)]
            send(ref, ref, ss.at[ch, at, k], sr.at[ch, (at - dx) % 4, k], dev(dx=dx, dc=dc))

    def near(ch):
        both(ch, slot_of(3, 0))
        both(ch, slot_of(1, 0))
        wait_e(ch, 6, 3, 1, PH)
        wait_e(ch, 8, 3, 1, NH)
        both(ch, slot_of(3, 1))
        share(ch, 0)
        share(ch, 3)
        wait_e(ch, 7, 1, 1, NH)
        wait_e(ch, 9, 1, 1, PH)
        both(ch, slot_of(1, 1))
        share(ch, 1)

    def far(ch):
        both(ch, slot_of(2, 0))
        wait_e(ch, 10, 2, 1, PH)
        wait_e(ch, 11, 2, 1, NH)
        both(ch, slot_of(2, 1))
        share(ch, 2)

    send_own(0)
    send(fac_ref.at[0], W.at[l], fs.at[0], fr.at[0], dev(lv=1 - l))
    send(AUX.at[l], AUX.at[l], fs.at[1], fr.at[1], dev(lv=1 - l))
    for ch in range(N_CH):
        send(emb_ref.at[pl.ds(ch * rc, rc), :], E.at[ch, j], es.at[ch, 12], er.at[ch, 12], to_c)
    for cp in local:
        cp.wait()
    WT[l] = W[l].T
    ready(l)
    for ch in range(N_CH):
        flip(ch, j)
        score(ch, j, l)
    for ch in range(N_CH):
        arrived(E.at[ch, slot_of(0, 1)], es.at[ch, 12], er.at[ch, 12])
        flip(ch, slot_of(0, 1))
        score(ch, slot_of(0, 1), l)

    def tell(k):
        for way, step in ((0, 1), (1, 7)):
            pl.semaphore_signal(ts.at[k, way], inc=1, device_id=dev(zv=(z + step) % NZ), device_id_type=MESH)

    def told(k):
        for way in (0, 1):
            pl.semaphore_wait(ts.at[k, way], 1)

    def soften(ch):
        s = S[ch]
        peak = jnp.max(jnp.max(s, axis=0), axis=0, keepdims=True)
        norm = jnp.sum(jnp.sum(jnp.exp(s - peak[None]), axis=0), axis=0, keepdims=True)
        mine = S[ch, :, :, lanes(j)]
        top = jnp.max(jnp.max(mine, axis=0), axis=0, keepdims=True)
        un = jnp.exp(mine - top[None])
        r = un / jnp.sum(jnp.sum(un, axis=0), axis=0, keepdims=True)[None]
        for xx in range(4):
            for cc in range(2):
                for ll in range(2):
                    k = xx * 4 + ll * 2 + cc
                    resp_ref[k : k + 1, pl.ds(ch * rc, rc)] = r[xx * 2 + cc, ll : ll + 1, :]
        return peak, norm

    def gather_moments(ch, lv, peak, norm):
        n = 8 * rc
        r = jnp.exp(S[ch, j, pl.ds(lv, 1), :] - peak) / norm
        for i in range(8):
            sl = slice(i * rc, (i + 1) * rc)
            ri = jnp.broadcast_to(r[:, sl], (8, rc))
            w = ET[ch, :, sl].astype(jnp.float32) * ri[0:1]
            hi = w.astype(jnp.bfloat16)
            WH[0:D, sl] = hi
            WL[0:D, sl] = (w - hi.astype(jnp.float32)).astype(jnp.bfloat16)
            r16 = jnp.concatenate([ri, ri], axis=0)
            rhi = r16.astype(jnp.bfloat16)
            WH[D : D + 16, sl] = rhi
            WL[D : D + 16, sl] = (r16 - rhi.astype(jnp.float32)).astype(jnp.bfloat16)
        left = E[ch, :, :, 0:256].reshape(n, 256)
        right = E[ch, :, :, 256:384].reshape(n, 128)
        a = jnp.dot(WH[...], left, preferred_element_type=jnp.float32)
        a = a + jnp.dot(WL[...], left, preferred_element_type=jnp.float32)
        d = jnp.dot(WH[256:400, :], right, preferred_element_type=jnp.float32)
        d = d + jnp.dot(WL[256:400, :], right, preferred_element_type=jnp.float32)
        row = lax.broadcasted_iota(jnp.int32, (128, 128), 0)
        col = lax.broadcasted_iota(jnp.int32, (128, 128), 1)
        d0, d1 = a[0:128, 0:128], a[128:256, 128:256]
        mixed = jnp.where(row >= col, d0, d1)
        diag = jnp.broadcast_to(jnp.sum(jnp.where(row == col, d1, 0.0), axis=0, keepdims=True), (8, 128))
        low = d[64:128, :]
        turn = jnp.where(row[0:64] >= col[0:64] - 64, pltpu.roll(d[0:64, :], 64, 1), low)
        pk = jnp.where(col[0:64] < 64, low, turn)
        diag2 = jnp.sum(jnp.where(row[0:64] == col[0:64] - 64, low, 0.0), axis=0, keepdims=True)
        diag2 = jnp.broadcast_to(diag2, (8, 128))
        cnt = jnp.broadcast_to(jnp.sum(r, axis=1, keepdims=True), (8, 128))
        sub = lax.broadcasted_iota(jnp.int32, (8, 128), 0)
        aux = jnp.where(
            sub == 0,
            a[D : D + 8, 0:128],
            jnp.where(sub == 1, a[D : D + 8, 128:256], jnp.where(sub == 2, d[128:136, :], jnp.where(sub == 3, cnt, jnp.where(sub == 4, diag, diag2)))),
        )
        parts = [
            (0, 0, a[128:D, 0:128]),
            (0, 256, pk[0:32]),
            (0, BODY, aux),
            (1, 0, a[256:D, 128:256]),
            (1, 128, mixed),
            (1, 256, pk[32:64]),
            (1, BODY, aux),
        ]
        for half, at, val in parts:
            where = pl.ds(at, val.shape[0])
            if ch == 0:
                M[lv, half, where, :] = val
            else:
                M[lv, half, where, :] = M[lv, half, where, :] + val

    tell(0)
    relay_first(0)
    told(0)
    tell(1)
    arrived(AUX.at[1 - l], fs.at[1], fr.at[1])
    arrived(W.at[1 - l], fs.at[0], fr.at[0])
    WT[1 - l] = W[1 - l].T
    ready(1 - l)
    for ch in range(N_CH):
        score(ch, j, 1 - l)
        score(ch, slot_of(0, 1), 1 - l)
    relay_second(0)
    told(1)
    tell(2)
    near(0)
    relay_first(1)
    told(2)
    relay_third(0)
    far(0)
    relay_second(1)
    near(1)
    relay_third(1)
    far(1)

    def wait_scores(ch):
        for at in (0, 1, 3, 2):
            for k, (dx, dc) in enumerate(group):
                arrived(S.at[ch, slot_of(-dx, dc), :, chip_lanes(at)], ss.at[ch, at, k], sr.at[ch, at, k])

    wait_scores(0)
    peak0, norm0 = soften(0)
    gather_moments(0, l, peak0, norm0)
    gather_moments(0, 1 - l, peak0, norm0)
    wait_scores(1)
    peak1, norm1 = soften(1)
    early = len(pending)
    A1, A2, B1, B2 = pl.ds(0, 96), pl.ds(96, 48), pl.ds(144, 96), pl.ds(240, 56)
    A, B = pl.ds(0, 144), pl.ds(144, PIECE - 144)
    gather_moments(1, l, peak1, norm1)
    for part, up, down in ((0, A1, B1), (1, A2, B2)):
        send(M.at[l, 1 - h, up, :], RY.at[up, :], ys.at[part], yr.at[part], ydev(yp))
        send(M.at[l, 1 - h, down, :], RY.at[down, :], ys.at[2 + part], yr.at[2 + part], ydev(ym))
    gather_moments(1, 1 - l, peak1, norm1)
    hp, hm = yp // 2, ym // 2
    send(M.at[1 - l, hp, B, :], F.at[0, B, :], ys.at[4], yr.at[4], ydev(yp))
    send(M.at[1 - l, hm, A, :], F.at[1, A, :], ys.at[5], yr.at[5], ydev(ym))
    drain(len(pending) - early)
    for part, up, down in ((0, A1, B1), (1, A2, B2)):
        arrived(RY.at[up, :], ys.at[part], yr.at[part])
        M[1 - l, hp, up, :] = M[1 - l, hp, up, :] + RY[up, :]
        send(M.at[1 - l, hp, up, :], F.at[0, up, :], ys.at[6 + part], yr.at[6 + part], ydev(yp))
        arrived(RY.at[down, :], ys.at[2 + part], yr.at[2 + part])
        M[1 - l, hm, down, :] = M[1 - l, hm, down, :] + RY[down, :]
        send(M.at[1 - l, hm, down, :], F.at[1, down, :], ys.at[8 + part], yr.at[8 + part], ydev(ym))

    def total(first, size):
        sl = slice(first, first + size)
        return M[l, h, sl, :] + F[0, sl, :] + F[1, sl, :]

    def along_z(part, Q, R):
        for dz in FAR_FIRST:
            zz = (z + dz) % NZ
            send(Q.at[zz], R.at[dz - 1], zs.at[part, dz - 1], zr.at[part, dz - 1], dev(zv=zz))

    def summed(part, Q, R):
        acc = Q[z]
        for dz in ORDER:
            arrived(R.at[dz - 1], zs.at[part, dz - 1], zr.at[part, dz - 1])
            acc = acc + R[dz - 1]
        return acc * scale

    over = dev(hv=1 - h)

    def spread(part, G):
        send(G.at[h, z], G.at[h, z], hs.at[part, 0], hr.at[part, 0], over)
        for dz in FAR_FIRST:
            send(G.at[h, z], G.at[h, z], gs.at[part, dz - 1], gr.at[part, dz - 1], dev(zv=(z + dz) % NZ))

    def cross(part, G):
        for dz in ORDER:
            zz = (z + NZ - dz) % NZ
            arrived(G.at[h, zz], gs.at[part, dz - 1], gr.at[part, dz - 1])
            send(G.at[h, zz], G.at[h, zz], hs.at[part, dz], hr.at[part, dz], over)

    arrived(F.at[0, B, :], ys.at[4], yr.at[4])
    arrived(F.at[1, A, :], ys.at[5], yr.at[5])
    arrived(F.at[0, A1, :], ys.at[6], yr.at[6])
    arrived(F.at[1, B1, :], ys.at[8], yr.at[8])
    for k in range(NZ):
        QZ0[k] = total((k // 4) * 144 + (k % 4) * Z0, Z0)
    along_z(0, QZ0, ZR0)
    arrived(F.at[0, A2, :], ys.at[7], yr.at[7])
    arrived(F.at[1, B2, :], ys.at[9], yr.at[9])
    tail = total(BODY, PIECE - BODY)
    for k in range(NZ):
        QZ1[k, 0:Z1, :] = total((k // 4) * 144 + 96 + (k % 4) * Z1, Z1)
        QZ1[k, Z1 : Z1 + 8, :] = tail
    along_z(1, QZ1, ZR1)
    G0[h, z] = summed(0, QZ0, ZR0)
    spread(0, G0)
    acc = summed(1, QZ1, ZR1)
    G1[h, z] = acc[0:Z1]
    FA[b] = acc[Z1 : Z1 + 8]
    spread(1, G1)
    blk_peers = [(dl, dx, dc) for dl in range(2) for dx in range(4) for dc in range(2)][1:]
    drain(2 * NZ)
    cross(0, G0)
    for k, (dl, dx, dc) in enumerate(blk_peers):
        send(FA.at[b], FA.at[b], bs.at[k], br.at[k], dev(dx=dx, dc=dc, lv=(l + dl) % 2))
    cross(1, G1)
    drain(2 * NZ)
    for k, (dl, dx, dc) in enumerate(blk_peers):
        bb = ((x - dx) % 4) * 4 + ((l + dl) % 2) * 2 + (c + dc) % 2
        arrived(FA.at[bb], bs.at[k], br.at[k])
    aux_ref[...] = FA[...]
    for part, G in ((0, G0), (1, G1)):
        for dz in range(NZ):
            arrived(G.at[1 - h, (z + NZ - dz) % NZ], hs.at[part, dz], hr.at[part, dz])
    for k in range(2):
        for t in range(NZ):
            at = (t // 4) * 144
            tri_ref[k, at + (t % 4) * Z0 : at + (t % 4 + 1) * Z0] = G0[k, t]
            tri_ref[k, at + 96 + (t % 4) * Z1 : at + 96 + (t % 4 + 1) * Z1] = G1[k, t]
    drain()


def finish(resp_in, aux_ref, tri_ref, resp_ref, counts_ref, first_ref, second_ref):
    b = lax.axis_index("blk")
    resp_ref[...] = resp_in[...]
    lane = lax.broadcasted_iota(jnp.int32, (1, 16), 1)
    counts = jnp.zeros((1, 16), jnp.float32)
    for k in range(16):
        counts = jnp.where(lane == k, aux_ref[k, 3:4, 0:16], counts)
        for t in range(3):
            first_ref[k : k + 1, t * 128 : (t + 1) * 128] = aux_ref[k, t : t + 1, :]
    counts_ref[...] = counts
    g0, g1 = tri_ref[0], tri_ref[1]
    row = lax.broadcasted_iota(jnp.int32, (128, 128), 0)
    col = lax.broadcasted_iota(jnp.int32, (128, 128), 1)
    mixed = g1[128:256]
    pk = jnp.concatenate([g0[256:288], g1[256:288]], axis=0)
    zero = jnp.zeros((64, 128), jnp.float32)
    low = jnp.concatenate([zero, pk], axis=0)
    high = jnp.concatenate([pltpu.roll(pk, 64, 1), zero], axis=0)
    low_t, high_t = low.T, high.T
    diag2 = aux_ref[b, 5:6, :]
    second_block = jnp.where(row < col, low, jnp.where(row > col, low_t, diag2))
    first_block = jnp.where(row >= col, high, high_t)
    bottom = jnp.where(col < 64, low, second_block)
    top = jnp.where(col < 64, first_block, low_t)
    corner = jnp.where(row < 64, top, bottom)
    turned = mixed.T
    diag = aux_ref[b, 4:5, :]
    second_ref[0, 0:128, 0:128] = jnp.where(row >= col, mixed, turned)
    second_ref[0, 128:384, 0:128] = g0[0:256]
    second_ref[0, 0:128, 128:256] = g0[0:128].T
    second_ref[0, 128:256, 128:256] = jnp.where(row < col, mixed, jnp.where(row > col, turned, diag))
    second_ref[0, 256:384, 128:256] = g1[0:128]
    second_ref[0, 0:128, 256:384] = g0[128:256].T
    second_ref[0, 128:256, 256:384] = g1[0:128].T
    second_ref[0, 256:384, 256:384] = corner


def shards(embeddings, factors, centres, log_prior):
    rows, width = embeddings.shape
    n_comp = factors.shape[0] * lax.axis_size("blk")
    n_rows = lax.axis_size("rows")
    scale = n_comp / (rows * lax.axis_size("blk") * n_rows)
    rc = rows // N_CH
    bf, f32 = jnp.bfloat16, jnp.float32
    vm = pl.BlockSpec(memory_space=pltpu.VMEM)
    dma = pltpu.SemaphoreType.DMA
    out = pltpu.VMEM
    any_ = pl.BlockSpec(memory_space=pltpu.HBM)
    resp, aux, tri = pl.pallas_call(
        functools.partial(kernel, scale),
        out_shape=(
            out((n_comp, rows), f32),
            out((n_comp, 8, 128), f32),
            out((2, BODY, 128), f32),
        ),
        in_specs=[any_] * 4,
        out_specs=(vm,) * 3,
        scratch_shapes=[
            pltpu.VMEM((N_CH, 8, rc, width), bf),
            pltpu.VMEM((N_CH, width, 8 * rc), bf),
            pltpu.VMEM((2, width, width), bf),
            pltpu.VMEM((2, width, width), bf),
            pltpu.VMEM((2, 8, width), f32),
            pltpu.VMEM((2, width, 128), f32),
            pltpu.VMEM((N_CH, 8, 2, 8 * rc), f32),
            pltpu.VMEM((width + 16, 8 * rc), bf),
            pltpu.VMEM((width + 16, 8 * rc), bf),
            pltpu.VMEM((2, 2, PIECE, 128), f32),
            pltpu.VMEM((PIECE, 128), f32),
            pltpu.VMEM((2, PIECE, 128), f32),
            pltpu.VMEM((NZ, Z0, 128), f32),
            pltpu.VMEM((NZ - 1, Z0, 128), f32),
            pltpu.VMEM((2, NZ, Z0, 128), f32),
            pltpu.VMEM((NZ, Z1 + 8, 128), f32),
            pltpu.VMEM((NZ - 1, Z1 + 8, 128), f32),
            pltpu.VMEM((2, NZ, Z1, 128), f32),
            pltpu.VMEM((16, 8, 128), f32),
            dma((N_CH, 13)),
            dma((N_CH, 13)),
            dma((2,)),
            dma((2,)),
            dma((N_CH, 4, 7)),
            dma((N_CH, 4, 7)),
            dma((10,)),
            dma((10,)),
            dma((2, NZ - 1)),
            dma((2, NZ - 1)),
            dma((2, NZ - 1)),
            dma((2, NZ - 1)),
            dma((2, NZ)),
            dma((2, NZ)),
            dma((15,)),
            dma((15,)),
            dma((N_CH + 3,)),
            pltpu.SemaphoreType.REGULAR((3, 2)),
            pltpu.VMEM((1, width), bf),
            pltpu.VMEM((1, 1), bf),
        ],
        compiler_params=pltpu.CompilerParams(
            collective_id=0, has_side_effects=True, vmem_limit_bytes=67043328 - 560 * 1024
        ),
    )(embeddings, factors, centres, log_prior.reshape(1, 1))
    resp, counts, first, second = pl.pallas_call(
        finish,
        out_shape=(
            jax.ShapeDtypeStruct((n_comp, rows), f32),
            jax.ShapeDtypeStruct((1, n_comp), f32),
            jax.ShapeDtypeStruct((n_comp, width), f32),
            jax.ShapeDtypeStruct((1, width, width), f32),
        ),
        in_specs=[vm] * 3,
        out_specs=(vm,) * 4,
        compiler_params=pltpu.CompilerParams(vmem_limit_bytes=8 * 1024 * 1024),
    )(resp, aux, tri)
    return (resp, counts.reshape(n_comp), first, second)


def solution(mesh):
    in_specs = (P(("blk", "rows"), None), P("blk", None, None), P("blk", None), P("blk"))
    out_specs = (P(None, ("blk", "rows")), P(), P(), P("blk", None, None))
    return jax.shard_map(shards, mesh=mesh, in_specs=in_specs, out_specs=out_specs, check_vma=False)
```
